32 devices in a mesh: gx: 4 (over z), gy: 2 (over x), gz: 4 (over y, core).
Axes of the slice: x: 2, y: 2, z: 4, core: 2. Of those that a mesh axis runs over, the one named last changes fastest.
Arguments:
- adj_final: float32 [4, 5, 64, 2048], P('gx', None, None, ('gy', 'gz')), may hold values from -6 to 6
- new_states: float32 [4, 3, 5, 64, 2048], P('gx', None, None, None, ('gy', 'gz')), may hold values from -1 to 4, as said below
- old_states: float32 [4, 3, 5, 64, 2048], P('gx', None, None, None, ('gy', 'gz')), may hold values from -1 to 4, as said below
- owner_device_index: int32 [4, 4096, 1], P('gx', ('gy', 'gz')), may hold values from 0 to 7; in each aligned block of 512 rows (0 to 511, 512 to 1023, ..., all dimensions but the last counted through in order) at most 128 rows name the same one
- owner_element_index: int32 [4, 4096], P('gx', ('gy', 'gz')), may hold values from 0 to 255
- proj_blocks: float32 [4, 64, 64, 4096], P('gx', None, None, ('gy', 'gz')), may hold values from -0.2 to 0.6
Outputs:
- adj_new: float32 [4, 5, 64, 2048], P('gx', None, None, ('gy', 'gz'))
- adj_old: float32 [4, 5, 64, 2048], P('gx', None, None, ('gy', 'gz'))
The draws below stay inside these ranges and needn't reach their ends.
Inputs may be any that keep to these rules, and one draw needn't show every extreme that they name: `owner_device_index`: in each aligned block of 512 slots (the slots of one device) no owner is named more than 128 times, a bound that some block reaches. `new_states`: variable 0 lies in 0.8 to 1.6, variables 1 to 3 in -1 to 1, variable 4 in 2.5 to 4. `old_states`: variable 0 lies in 0.8 to 1.6, variables 1 to 3 in -1 to 1, variable 4 in 2.5 to 4.
All inputs are finite; a program needn't handle non-finite values.
Results may differ from the reference program's by a relative error of at most 0.0003.
Values sent between devices are 32-bit elements; how exact they have to be, the bound alone decides.
No kernel may reach another device: no remote copies, remote signals or barrier semaphores. Data moves between devices by JAX's collectives and lax.ppermute only.
A program may use at most 128 MiB of HBM per device.

```python
import math
import jax
import jax.numpy as jnp
import numpy as np
from jax import lax

NVAR = 5
ELEMENT_NODES = 64
ELEMENTS_Z = 64
ELEMENTS_X = 4
NYZ = 2048
ELEMENTS_LOCAL = 256
LOCAL_SLOTS = 512
PLANE_SLOTS = 4096
OWNER_SLOT_LIMIT = 128
N_GY = 2
N_GZ = 4


def state_draw(key):
    random_subkeys = jax.random.split(key, 3)
    one_shape = (ELEMENTS_X, 3, 1, ELEMENT_NODES, NYZ)
    moment_shape = (ELEMENTS_X, 3, 3, ELEMENT_NODES, NYZ)
    density = jax.random.uniform(random_subkeys[0], one_shape, jnp.float32, 0.8, 1.6)
    energy = jax.random.uniform(random_subkeys[2], one_shape, jnp.float32, 2.5, 4.0)
    moments = jnp.clip(0.3 * jax.random.normal(random_subkeys[1], moment_shape, jnp.float32), -1.0, 1.0)
    return jnp.concatenate([density, moments, energy], axis=2)


def draw_new_states(key, part):
    return state_draw(jax.random.fold_in(key, 101))


def draw_old_states(key, part):
    return state_draw(jax.random.fold_in(key, 202))


def draw_proj_blocks(key, part):
    random_subkeys = jax.random.split(jax.random.fold_in(key, 303), 2)
    complete_shape = (ELEMENTS_X, ELEMENT_NODES, ELEMENT_NODES, PLANE_SLOTS)
    spread = jnp.clip(0.04 * jax.random.normal(random_subkeys[0], complete_shape, jnp.float32), -0.2, 0.2)
    diagonal_part = jax.random.uniform(random_subkeys[1], (ELEMENTS_X, 1, ELEMENT_NODES, PLANE_SLOTS), jnp.float32, 0.2, 0.6)
    on_diag = (jnp.arange(ELEMENT_NODES)[:, None] == jnp.arange(ELEMENT_NODES)[None, :])[None, :, :, None]
    return jnp.where(on_diag, diagonal_part, spread)


def place_ends(values, own_key, low, high):
    shape = values.shape
    spot = [jax.random.randint(jax.random.fold_in(own_key, axis), (), 0, shape[axis]) for axis in range(len(shape))]
    values = values.at[tuple(spot)].set(low)
    longest = shape.index(max(shape))
    spot[longest] = (spot[longest] + 1) % shape[longest]
    return values.at[tuple(spot)].set(high)


def level_of(stream_key, extent, cuts, smallest, top_value):
    def one(dim, blocks):
        steps = jax.random.uniform(jax.random.fold_in(jax.random.fold_in(stream_key, 6), dim), (blocks,), jnp.float32, smallest / len(cuts), top_value / len(cuts))
        return jnp.repeat(jnp.exp(steps), extent[dim] // blocks).reshape((-1,) + (1,) * (len(extent) - dim - 1))

    level = one(*cuts[0])
    for cut in cuts[1:]:
        level = level * one(*cut)
    return level


def shared_out(key, own, number, rows, amount, top, reach, lean):
    sequence = jax.random.permutation(key, amount)
    crowded, common = portions_of(amount, rows * top, reach, lean, True), portions_of(amount, rows * top, reach, lean, False)
    places = jnp.arange(amount)

    def named(sizes, offset_by):
        used = int((sizes > 0).sum())
        fixed = max(1, used // 4)
        moved = fixed + (places - fixed + offset_by * (used - fixed)) % max(1, amount - fixed)
        return jnp.zeros((amount,), jnp.int32).at[sequence[jnp.where(places < fixed, places, moved)]].set(jnp.asarray(sizes, jnp.int32))

    sizes = jnp.where(number % 4 == 0, named(crowded, number // 4), named(common, number - number // 4 - 1))
    mixed = jax.random.permutation(jax.random.fold_in(own, 3), amount)
    source_of, receiver = mixed[0:amount // 2 * 2:2], mixed[1:amount // 2 * 2:2]
    slack = jnp.minimum(sizes[source_of] - 1, reach - sizes[receiver]) // 2
    slack = jnp.where((source_of == sequence[0]) | (receiver == sequence[0]) | (sizes[receiver] == 0), 0, jnp.maximum(slack, 0))
    moved = jax.random.randint(jax.random.fold_in(own, 4), (amount // 2,), 0, 1 << 20) % (slack + 1)
    sizes = sizes.at[source_of].add(-moved).at[receiver].add(moved)
    members = jnp.searchsorted(jnp.cumsum(sizes), jnp.arange(rows * top), side="right").astype(jnp.int32)
    listing = members.reshape(top, rows).T
    listing = listing[jax.random.permutation(jax.random.fold_in(own, 1), rows)]
    offset_by = jax.random.randint(jax.random.fold_in(own, 2), (rows, 1), 0, top)
    return jnp.take_along_axis(listing, (jnp.arange(top)[None, :] + offset_by) % top, axis=1)


def portions_of(amount, total, most, skew, full):
    weights = [(1 << 20) // math.isqrt(grade ** skew) + 1 for grade in range(1, amount + 1)]
    largest = most if full else min(most, max(-(-total // amount), total * weights[0] // sum(weights)))
    least = 1 if total - largest >= amount - 1 else 0
    given, rest = [largest] + [least] * (amount - 1), total - largest - least * (amount - 1)
    while rest > 0:
        free = [i for i in range(1, amount) if given[i] < largest] or [i for i in range(1, amount) if given[i] < most]
        pool, budget = sum([weights[i] for i in free]), rest
        for i in free:
            more = min(most - given[i], max(1, budget * weights[i] // pool), rest)
            given[i] = given[i] + more
            rest = rest - more
    return np.array(given)


def centred(key, dims, scale, most, shards=(), kind=jnp.bfloat16):
    entries = jax.random.normal(key, dims, jnp.float32) * scale
    if len(shards) > 0:
        entries = level_of(key, dims, shards, -0.22, 0.18) * entries
    return jnp.clip(entries, min=-most, max=most).astype(kind)


def setup_inputs(seed: int = 0) -> dict:
    keys = jax.random.split(jax.random.key(seed), 7)
    adj_final = centred(keys[0], (ELEMENTS_X, NVAR, ELEMENT_NODES, NYZ), 1.0, 6.0, ((0, 4), (3, 8)), jnp.float32)
    new_states = draw_new_states(jax.random.fold_in(keys[6], 71), 0)
    old_states = draw_old_states(jax.random.fold_in(keys[6], 71), 0)
    owner_device_index_keys = jax.random.split(jax.random.fold_in(keys[3], 1), ELEMENTS_X * PLANE_SLOTS // LOCAL_SLOTS)
    owner_device_index_turns = jax.random.permutation(jax.random.fold_in(keys[3], 3), ELEMENTS_X * PLANE_SLOTS // LOCAL_SLOTS)
    owner_device_index = jax.vmap(lambda own, number: shared_out(jax.random.fold_in(keys[3], 2), own, number, LOCAL_SLOTS, N_GY * N_GZ, 1, OWNER_SLOT_LIMIT, 2))(owner_device_index_keys, owner_device_index_turns).reshape((ELEMENTS_X, PLANE_SLOTS, 1))
    owner_element_index = place_ends(jax.random.randint(keys[4], (ELEMENTS_X, PLANE_SLOTS), 0, ELEMENTS_LOCAL), jax.random.fold_in(keys[4], 1), 0, ELEMENTS_LOCAL - 1).astype(jnp.int32)
    proj_blocks = draw_proj_blocks(jax.random.fold_in(keys[6], 71), 0)
    return {"adj_final": adj_final, "new_states": new_states, "old_states": old_states, "owner_device_index": owner_device_index, "owner_element_index": owner_element_index, "proj_blocks": proj_blocks}


heat_ratio = 1.4
step_rate = 0.01
lift_scale = 6.0
highest = lax.Precision.HIGHEST

def lgl_matrix():
    points = np.array([-1.0, -1.0 / np.sqrt(5.0), 1.0 / np.sqrt(5.0), 1.0])
    factors = np.array([np.prod([points[i] - points[j] for j in range(4) if j != i]) for i in range(4)])
    deriv_table = np.zeros((4, 4))
    for i in range(4):
        for j in range(4):
            if i != j:
                deriv_table[i, j] = factors[i] / (factors[j] * (points[i] - points[j]))
    for i in range(4):
        deriv_table[i, i] = -np.sum(deriv_table[i])
    return deriv_table

def euler_fluxes(fields):
    density = fields[0]
    moments = fields[1:4]
    energy = fields[4]
    speeds = moments / density
    pressure = (heat_ratio - 1.0) * (energy - 0.5 * lax.optimization_barrier(jnp.sum(moments * speeds, axis=0)))
    output = []
    for direction in range(3):
        pieces = [moments[direction]]
        for component in range(3):
            mom_flux = moments[component] * speeds[direction]
            if component == direction:
                mom_flux = mom_flux + pressure
            pieces.append(mom_flux)
        pieces.append(speeds[direction] * (energy + pressure))
        output.append(jnp.stack(pieces))
    return tuple(output)

def add_faces(values_in, face_axis, low_add, high_add):
    bottom_row = lax.slice_in_dim(values_in, 0, 1, axis=face_axis) + jnp.expand_dims(low_add, face_axis)
    middle = lax.slice_in_dim(values_in, 1, 3, axis=face_axis)
    top_row = lax.slice_in_dim(values_in, 3, 4, axis=face_axis) + jnp.expand_dims(high_add, face_axis)
    return jnp.concatenate([bottom_row, middle, top_row], axis=face_axis)

def section_adjoint(fields, adjoint, table, neighbours):
    derivs = [jnp.einsum('li,vljkxe->vijkxe', table, adjoint, precision=highest), jnp.einsum('lj,vilkxe->vijkxe', table, adjoint, precision=highest), jnp.einsum('lk,vijlxe->vijkxe', table, adjoint, precision=highest)]
    cotangents = []
    penalty = jnp.zeros_like(adjoint)
    for direction in range(3):
        face_axis = direction + 1
        lower_face = lax.index_in_dim(adjoint, 0, face_axis, keepdims=False)
        upper_face = lax.index_in_dim(adjoint, 3, face_axis, keepdims=False)
        lower_incoming, upper_incoming = neighbours(direction, adjoint, lower_face, upper_face)
        own_low = lift_scale * lower_face
        own_high = lift_scale * upper_face
        received_low = lift_scale * lower_incoming
        received_high = lift_scale * upper_incoming
        cotangents.append(add_faces(derivs[direction], face_axis, 0.5 * (received_low + own_low), -0.5 * (own_high + received_high)))
        penalty = add_faces(penalty, face_axis, own_low - received_low, own_high - received_high)
    unused, pullback = jax.vjp(euler_fluxes, fields)
    gradient, = pullback(tuple(cotangents))
    return -step_rate * (gradient + penalty)

def reverse_step(section_fields, adjoint, table, neighbours):
    second = 2.0 / 3.0 * (adjoint + section_adjoint(section_fields[2], adjoint, table, neighbours))
    earlier = 0.25 * (second + section_adjoint(section_fields[1], second, table, neighbours))
    return adjoint / 3.0 + 0.75 * second + earlier + section_adjoint(section_fields[0], earlier, table, neighbours)

def global_faces(direction, adjoint, lower_face, upper_face):
    if direction == 0:
        return (jnp.roll(upper_face, 1, axis=3), jnp.roll(lower_face, -1, axis=3))
    if direction == 1:
        return (jnp.roll(upper_face, ELEMENTS_Z, axis=4), jnp.roll(lower_face, -ELEMENTS_Z, axis=4))
    depth_position = jnp.arange(lower_face.shape[4]) % ELEMENTS_Z
    lower_incoming = jnp.where(depth_position == 0, jnp.roll(upper_face, 1 - ELEMENTS_Z, axis=4), jnp.roll(upper_face, 1, axis=4))
    upper_incoming = jnp.where(depth_position == ELEMENTS_Z - 1, jnp.roll(lower_face, ELEMENTS_Z - 1, axis=4), jnp.roll(lower_face, -1, axis=4))
    return (lower_incoming, upper_incoming)

def reference(adj_final, new_states, old_states, owner_device_index, owner_element_index, proj_blocks):
    table = jnp.asarray(lgl_matrix(), jnp.float32)
    final_moved = jnp.moveaxis(adj_final, 0, 2)
    new_moved = jnp.moveaxis(new_states, 0, 3)
    old_moved = jnp.moveaxis(old_states, 0, 3)
    blocks_moved = jnp.moveaxis(proj_blocks, 0, 2)
    grid_shape = (NVAR, 4, 4, 4, ELEMENTS_X, NYZ)
    begin_adj = final_moved.reshape(grid_shape)
    adj_new = reverse_step(new_moved.reshape((3,) + grid_shape), begin_adj, table, global_faces)
    adj_new = adj_new.reshape(final_moved.shape)
    slot_position = jnp.arange(PLANE_SLOTS).astype(jnp.int32)
    source = (slot_position // LOCAL_SLOTS * ELEMENTS_LOCAL + slot_position % ELEMENTS_LOCAL).astype(jnp.int32)

    def project_plane(plane):
        blocks = lax.dynamic_index_in_dim(blocks_moved, plane, 2, keepdims=False)
        values = lax.dynamic_index_in_dim(adj_new, plane, 2, keepdims=False)
        gathered = jnp.take(values, source, axis=2)
        products = jnp.einsum('nmr,vnr->vmr', blocks, gathered, precision=highest)
        owners = lax.dynamic_index_in_dim(owner_device_index, plane, 0, keepdims=False)[:, 0]
        locals_in = lax.dynamic_index_in_dim(owner_element_index, plane, 0, keepdims=False)
        target = (owners * ELEMENTS_LOCAL + locals_in).astype(jnp.int32)
        return jnp.zeros(values.shape, values.dtype).at[:, :, target].add(products)
    planes = lax.map(project_plane, jnp.arange(ELEMENTS_X).astype(jnp.int32))
    adj_proj = jnp.moveaxis(planes, 0, 2)
    adj_old = reverse_step(old_moved.reshape((3,) + grid_shape), adj_proj.reshape(grid_shape), table, global_faces)
    adj_old = adj_old.reshape(final_moved.shape)
    return (jnp.moveaxis(adj_new, 2, 0), jnp.moveaxis(adj_old, 2, 0))
```

```python
import functools

import jax
import jax.numpy as jnp
import numpy as np
from jax import lax
from jax.experimental import pallas as pl
from jax.experimental.pallas import tpu as pltpu
from jax.sharding import PartitionSpec as P

ELEMENTS_Z = 64

step_rate = 0.01
lift_scale = 6.0
half_lift = 3.0
vmem_limit = 40 * 1024 * 1024
VARS = 5
LANES = 128


def shifted(value, axis, steps):
    count = lax.axis_size(axis)
    pairs = [(source, (source + steps) % count) for source in range(count)]
    return lax.ppermute(value, axis, pairs)


def lgl_matrix():
    points = np.array([-1.0, -1.0 / np.sqrt(5.0), 1.0 / np.sqrt(5.0), 1.0])
    factors = np.array(
        [np.prod([points[i] - points[j] for j in range(4) if j != i]) for i in range(4)]
    )
    deriv_table = np.zeros((4, 4))
    for i in range(4):
        for j in range(4):
            if i != j:
                deriv_table[i, j] = factors[i] / (factors[j] * (points[i] - points[j]))
    for i in range(4):
        deriv_table[i, i] = -np.sum(deriv_table[i])
    return deriv_table


face_table = lgl_matrix()
face_table[0, 0] += half_lift
face_table[3, 3] -= half_lift
assert np.max(np.abs(np.diag(face_table))) < 1e-12


def iotas():
    row = lax.broadcasted_iota(jnp.int32, (8, LANES), 0)
    lane = lax.broadcasted_iota(jnp.int32, (8, LANES), 1)
    return row, lane


def by_sublane(row, values):
    out = jnp.full((8, LANES), np.float32(values[7]))
    for s in range(6, -1, -1):
        out = jnp.where(row == s, np.float32(values[s]), out)
    return out


def tile_of(ref, v, i, j):
    return ref[v, 8 * i : 8 * i + 8, LANES * j : LANES * (j + 1)]


def primitive_state(get):
    inverse = 1.0 / get(0)
    speeds = [get(1 + d) * inverse for d in range(3)]
    kinetic = (
        get(1) * speeds[0] + get(2) * speeds[1] + get(3) * speeds[2]
    )
    energy = get(4)
    pressure = 0.4 * (energy - 0.5 * kinetic)
    return speeds, (energy + pressure) * inverse


def pull_full(speeds, enthalpy, v):
    total = v[0][4] * speeds[0] + v[1][4] * speeds[1] + v[2][4] * speeds[2]
    weight = v[0][1] + v[1][2] + v[2][3] + total
    fifth = 0.2 * weight
    pulled = []
    for d in range(3):
        part = (
            v[d][1] * speeds[0]
            + v[d][2] * speeds[1]
            + v[d][3] * speeds[2]
            + v[d][4] * enthalpy
        )
        pulled.append(part - fifth * speeds[d])
    out = [-(pulled[0] * speeds[0] + pulled[1] * speeds[1] + pulled[2] * speeds[2])]
    for j in range(3):
        moved = (
            v[0][1 + j] * speeds[0] + v[1][1 + j] * speeds[1] + v[2][1 + j] * speeds[2]
        )
        out.append(v[j][0] + moved - fifth * speeds[j] + pulled[j])
    out.append(total + 2.0 * fifth)
    return out


def pull_one(direction, speeds, enthalpy, v):
    own = speeds[direction]
    total = v[4] * own
    fifth = 0.2 * (v[1 + direction] + total)
    pulled = [-fifth * speeds[d] for d in range(3)]
    pulled[direction] = (
        v[1] * speeds[0]
        + v[2] * speeds[1]
        + v[3] * speeds[2]
        + v[4] * enthalpy
        + pulled[direction]
    )
    out = [-(pulled[0] * speeds[0] + pulled[1] * speeds[1] + pulled[2] * speeds[2])]
    for j in range(3):
        moved = v[1 + j] * own - fifth * speeds[j] + pulled[j]
        out.append(v[0] + moved if j == direction else moved)
    out.append(total + 2.0 * fifth)
    return out


def local_kernel(scale, extras, halves, *refs):
    state_ref, w_ref = refs[0], refs[1]
    extra_refs = refs[2 : 2 + len(extras)]
    out_ref = refs[2 + len(extras)]
    row, lane = iotas()
    low_half_rows = row < 4
    low_half_lanes = lane < 64
    within = row % 4
    z_first = lane % ELEMENTS_Z == 0
    z_last = lane % ELEMENTS_Z == ELEMENTS_Z - 1
    z_shift = {}
    for k in (1, 2, 3, -1, -2, -3):
        column = [
            face_table[s % 4 - k, s % 4] if 0 <= s % 4 - k <= 3 else 0.0 for s in range(8)
        ]
        z_shift[k] = by_sublane(row, column)
    z_low = by_sublane(row, [half_lift if s % 4 == 0 else 0.0 for s in range(8)])
    z_high = by_sublane(row, [-half_lift if s % 4 == 3 else 0.0 for s in range(8)])
    zero = jnp.zeros((8, LANES), jnp.float32)

    for j in range(halves):
        for i in range(8):
            a, t = i // 2, i % 2
            other = 2 * a + 1 - t
            bs = [2 * t + s // 4 for s in range(8)]
            y_same = by_sublane(row, [face_table[2 * (1 - t) + s // 4, bs[s]] for s in range(8)])
            y_swap = by_sublane(row, [face_table[2 * t + 1 - s // 4, bs[s]] for s in range(8)])
            y_both = by_sublane(
                row, [face_table[2 * (1 - t) + 1 - s // 4, bs[s]] for s in range(8)]
            )
            y_face_rows = low_half_rows if t == 0 else jnp.logical_not(low_half_rows)
            y_sign = half_lift if t == 0 else -half_lift
            y_face = jnp.where(y_face_rows, np.float32(y_sign), 0.0)
            count = by_sublane(
                row,
                [
                    lift_scale
                    * ((a in (0, 3)) + (bs[s] in (0, 3)) + (s % 4 in (0, 3)))
                    for s in range(8)
                ],
            )
            v = [[], [], []]
            penalties = []
            for var in range(VARS):
                w = tile_of(w_ref, var, i, j)
                acc = None
                for source in range(4):
                    if source == a:
                        continue
                    term = np.float32(face_table[source, a]) * tile_of(
                        w_ref, var, 2 * source + t, j
                    )
                    acc = term if acc is None else acc + term
                v[0].append(acc)
                pair = tile_of(w_ref, var, other, j)
                pair_swapped = pltpu.roll(pair, 4, 0)
                acc = (
                    y_same * pair
                    + y_swap * pltpu.roll(w, 4, 0)
                    + y_both * pair_swapped
                )
                here = pltpu.roll(pair_swapped, 64, 1)
                if t == 0:
                    before = (
                        pltpu.roll(pltpu.roll(tile_of(w_ref, var, other, j - 1), 4, 0), 64, 1)
                        if j > 0
                        else zero
                    )
                    y_in = jnp.where(low_half_lanes, before, here)
                else:
                    after = (
                        pltpu.roll(pltpu.roll(tile_of(w_ref, var, other, j + 1), 4, 0), 64, 1)
                        if j < halves - 1
                        else zero
                    )
                    y_in = jnp.where(low_half_lanes, here, after)
                y_term = y_face * y_in
                v[1].append(acc + y_term)
                acc = None
                moved = {}
                for k in (1, 2, 3, -1, -2, -3):
                    moved[k] = pltpu.roll(w, k % 8, 0)
                    term = z_shift[k] * moved[k]
                    acc = term if acc is None else acc + term
                below = jnp.where(
                    z_first, pltpu.roll(moved[-3], 65, 1), pltpu.roll(moved[-3], 1, 1)
                )
                above = jnp.where(
                    z_last, pltpu.roll(moved[3], 63, 1), pltpu.roll(moved[3], 127, 1)
                )
                low_term = z_low * below
                high_term = z_high * above
                v[2].append(acc + low_term + high_term)
                y_jump = y_term if t == 0 else -y_term
                penalties.append(
                    count * w - 2.0 * (y_jump + (low_term - high_term))
                )
            speeds, enthalpy = primitive_state(lambda q: tile_of(state_ref, q, i, j))
            pulled = pull_full(speeds, enthalpy, v)
            for var in range(VARS):
                change = (-step_rate * scale) * (pulled[var] + penalties[var])
                base = scale * tile_of(w_ref, var, i, j)
                for ref, factor in zip(extra_refs, extras):
                    base = base + np.float32(factor) * tile_of(ref, var, i, j)
                out_ref[var, 8 * i : 8 * i + 8, LANES * j : LANES * (j + 1)] = base + change


def pack_faces(w_ref, halves, xl_ref, xu_ref, yl_ref, yu_ref):
    row, lane = iotas()
    low_rows = row < 4
    low_lanes = lane < 64
    for var in range(VARS):
        xl_ref[var] = w_ref[var, 0:16, :]
        xu_ref[var] = w_ref[var, 48:64, :]
        low = [tile_of(w_ref, var, 2 * a, 0) for a in range(4)]
        left = jnp.where(low_rows, low[0], pltpu.roll(low[1], 4, 0))
        right = jnp.where(low_rows, low[2], pltpu.roll(low[3], 4, 0))
        yl_ref[var] = jnp.where(low_lanes, left, pltpu.roll(right, 64, 1))
        high = [tile_of(w_ref, var, 2 * a + 1, halves - 1) for a in range(4)]
        left = jnp.where(low_rows, pltpu.roll(high[0], 4, 0), high[1])
        right = jnp.where(low_rows, pltpu.roll(high[2], 4, 0), high[3])
        yu_ref[var] = jnp.where(low_lanes, pltpu.roll(left, 64, 1), right)


def face_kernel(halves, w_ref, *out_refs):
    pack_faces(w_ref, halves, *out_refs)


def finish_kernel(
    scale, with_faces, halves, state_ref, base_ref, xlow_ref, xhigh_ref, ylow_ref, yhigh_ref, *outs
):
    out_ref = outs[0]
    row, lane = iotas()
    rate = np.float32(-step_rate * scale)
    y_low_mask = jnp.where(jnp.logical_and(row < 4, lane < 64), np.float32(half_lift), 0.0)
    y_high_mask = jnp.where(jnp.logical_and(row >= 4, lane >= 64), np.float32(-half_lift), 0.0)
    for j in range(halves):
        for i in range(8):
            a, t = i // 2, i % 2
            has_x = a in (0, 3)
            has_y = (t == 0 and j == 0) or (t == 1 and j == halves - 1)
            place = (slice(8 * i, 8 * i + 8), slice(LANES * j, LANES * (j + 1)))
            values = [base_ref[(var,) + place] for var in range(VARS)]
            if has_x or has_y:
                speeds, enthalpy = primitive_state(lambda q: tile_of(state_ref, q, i, j))
            if has_x:
                source = xlow_ref if a == 0 else xhigh_ref
                sign = half_lift if a == 0 else -half_lift
                got = [np.float32(sign) * tile_of(source, var, t, j) for var in range(VARS)]
                pulled = pull_one(0, speeds, enthalpy, got)
                jump = 2.0 if a == 0 else -2.0
                values = [
                    x + rate * (g - jump * q) for x, g, q in zip(values, pulled, got)
                ]
            if has_y:
                got = []
                for var in range(VARS):
                    packed = (ylow_ref if t == 0 else yhigh_ref)[var]
                    if t == 0:
                        if a >= 2:
                            packed = pltpu.roll(packed, 64, 1)
                        if a % 2 == 1:
                            packed = pltpu.roll(packed, 4, 0)
                        got.append(y_low_mask * packed)
                    else:
                        if a < 2:
                            packed = pltpu.roll(packed, 64, 1)
                        if a % 2 == 0:
                            packed = pltpu.roll(packed, 4, 0)
                        got.append(y_high_mask * packed)
                pulled = pull_one(1, speeds, enthalpy, got)
                jump = 2.0 if t == 0 else -2.0
                values = [
                    x + rate * (g - jump * q) for x, g, q in zip(values, pulled, got)
                ]
            for var in range(VARS):
                out_ref[(var,) + place] = values[var]
    if with_faces:
        pack_faces(out_ref, halves, *outs[1:])


def vmem_spec():
    return pl.BlockSpec(memory_space=pltpu.VMEM)


def params():
    return pltpu.CompilerParams(vmem_limit_bytes=vmem_limit)


def face_shapes(columns):
    return [
        jax.ShapeDtypeStruct((VARS, 16, columns), jnp.float32),
        jax.ShapeDtypeStruct((VARS, 16, columns), jnp.float32),
        jax.ShapeDtypeStruct((VARS, 8, LANES), jnp.float32),
        jax.ShapeDtypeStruct((VARS, 8, LANES), jnp.float32),
    ]


def get_faces(w):
    columns = w.shape[2]
    return pl.pallas_call(
        functools.partial(face_kernel, columns // LANES),
        out_shape=face_shapes(columns),
        in_specs=[vmem_spec()],
        out_specs=[vmem_spec()] * 4,
        compiler_params=params(),
        name="faces",
    )(w)


def exchange(faces):
    xl, xu, yl, yu = faces
    x_low = shifted(xu, "gx", 1)
    x_high = shifted(xl, "gx", -1)
    y_low = shifted(yu, ("gy", "gz"), 1)
    y_high = shifted(yl, ("gy", "gz"), -1)
    return x_low, x_high, y_low, y_high


def section(states, index, w, faces, scale, extras, with_faces):
    columns = w.shape[2]
    halves = columns // LANES
    shape = jax.ShapeDtypeStruct(w.shape, jnp.float32)
    received = exchange(faces)
    state = states[index]
    base = pl.pallas_call(
        functools.partial(local_kernel, scale, tuple(f for _, f in extras), halves),
        out_shape=shape,
        in_specs=[vmem_spec()] * (2 + len(extras)),
        out_specs=vmem_spec(),
        compiler_params=params(),
        cost_estimate=pl.CostEstimate(
            flops=400 * 64 * columns, bytes_accessed=12 * VARS * 64 * columns, transcendentals=0
        ),
        name="local_part",
    )(state, w, *[x for x, _ in extras])
    out_shape = [shape] + (face_shapes(columns) if with_faces else [])
    return pl.pallas_call(
        functools.partial(finish_kernel, scale, with_faces, halves),
        out_shape=out_shape,
        in_specs=[vmem_spec()] * 6,
        out_specs=[vmem_spec()] * len(out_shape),
        compiler_params=params(),
        name="finish",
    )(state, base, *received)


def reverse_step(states, begin, faces):
    second, *faces = section(states, 2, begin, faces, 2.0 / 3.0, [], True)
    first, *faces = section(states, 1, second, faces, 0.25, [], True)
    (result,) = section(
        states, 0, first, faces, 1.0, [(begin, 1.0 / 3.0), (second, 0.75)], False
    )
    return result


def split_three(x):
    high = x.astype(jnp.bfloat16)
    rest = x - high.astype(jnp.float32)
    middle = rest.astype(jnp.bfloat16)
    low = (rest - middle.astype(jnp.float32)).astype(jnp.bfloat16)
    return high, middle, low


def project_kernel(m_tiles, w_ref, block_ref, placing_ref, extra_ref, out_ref, held):
    step = pl.program_id(0)

    def body(n, sums):
        sums = list(sums)
        rows = [
            jnp.broadcast_to(w_ref[var, pl.ds(n, 1), :], (8, LANES)) for var in range(VARS)
        ]
        for m in range(m_tiles):
            block = block_ref[n, 8 * m : 8 * m + 8, :]
            for var in range(VARS):
                q = m * VARS + var
                sums[q] = sums[q] + block * rows[var]
        return tuple(sums)

    start = tuple(jnp.zeros((8, LANES), jnp.float32) for _ in range(m_tiles * VARS))
    sums = lax.fori_loop(0, 64, body, start, unroll=8)
    for q in range(m_tiles * VARS):
        held[step, 8 * q : 8 * q + 8, :] = sums[q]

    @pl.when(step == pl.num_programs(0) - 1)
    def _():
        total = m_tiles * VARS * 8
        result = jnp.zeros((total + 8, placing_ref.shape[1]), jnp.float32)
        for s in range(held.shape[0]):
            values = jnp.concatenate([held[s], extra_ref[:, LANES * s : LANES * (s + 1)]], axis=0)
            spot = placing_ref[LANES * s : LANES * (s + 1), :]
            for piece in split_three(values):
                result = result + jnp.dot(piece, spot, preferred_element_type=jnp.float32)
        for g in range(out_ref.shape[0]):
            out_ref[g] = result[:, LANES * g : LANES * (g + 1)]


def project(w, blocks, placing, extra, first, m_tiles):
    halves = w.shape[2] // LANES
    slots = blocks.shape[3]
    steps = slots // LANES
    rows = m_tiles * VARS * 8
    places = placing.shape[1]
    return pl.pallas_call(
        functools.partial(project_kernel, m_tiles),
        out_shape=jax.ShapeDtypeStruct((places // LANES, rows + 8, LANES), jnp.float32),
        grid=(steps,),
        in_specs=[
            pl.BlockSpec((VARS, 64, LANES), lambda s: (0, 0, lax.rem(s, halves))),
            pl.BlockSpec((None, 64, 8 * m_tiles, LANES), lambda s: (0, 0, first, s)),
            vmem_spec(),
            vmem_spec(),
        ],
        out_specs=vmem_spec(),
        scratch_shapes=[pltpu.VMEM((steps, rows, LANES), jnp.float32)],
        compiler_params=params(),
        name="project",
    )(w, blocks, placing, extra)


def receive_kernel(count, m_tiles, halves, *refs):
    incoming = refs[:count]
    out_ref = refs[count]
    columns = out_ref.shape[2]
    spots = []
    for g in range(incoming[0].shape[0]):
        rows = m_tiles * VARS * 8
        local = incoming[0][g, rows : rows + 1, :].astype(jnp.int32)
        index = lax.broadcasted_iota(jnp.int32, (columns, LANES), 0)
        spots.append((index == local).astype(jnp.float32).astype(jnp.bfloat16))
    for piece_index in range(count):
        rows = m_tiles * VARS * 8
        result = jnp.zeros((rows, columns), jnp.float32)
        for g, spot in enumerate(spots):
            for piece in split_three(incoming[piece_index][g, 0:rows, :]):
                result = result + lax.dot_general(
                    piece, spot, (((1,), (1,)), ((), ())), preferred_element_type=jnp.float32
                )
        for m in range(m_tiles):
            node = 8 * (piece_index * m_tiles + m)
            for var in range(VARS):
                q = m * VARS + var
                out_ref[var, node : node + 8, :] = result[8 * q : 8 * q + 8, :]
    pack_faces(out_ref, halves, *refs[count + 1 :])


def receive(incoming, columns, m_tiles):
    shapes = [jax.ShapeDtypeStruct((VARS, 64, columns), jnp.float32)] + face_shapes(columns)
    return pl.pallas_call(
        functools.partial(receive_kernel, len(incoming), m_tiles, columns // LANES),
        out_shape=shapes,
        in_specs=[vmem_spec()] * len(incoming),
        out_specs=[vmem_spec()] * len(shapes),
        compiler_params=params(),
        name="receive",
    )(*incoming)


def send_to_owners(values, group, capacity):
    blocks, rows, lanes = values.shape
    if capacity == lanes:
        return lax.all_to_all(values, ("gy", "gz"), split_axis=0, concat_axis=0, tiled=True)
    per = lanes // capacity
    values = values.reshape(blocks, rows, per, capacity).transpose(0, 2, 1, 3)
    values = values.reshape(group, rows, capacity)
    values = lax.all_to_all(values, ("gy", "gz"), split_axis=0, concat_axis=0, tiled=True)
    values = values.reshape(blocks, per, rows, capacity).transpose(0, 2, 1, 3)
    return values.reshape(blocks, rows, lanes)


CHUNKS = 1


def per_device(
    adj_final, new_states, old_states, owner_device_index, owner_element_index, proj_blocks
):
    columns = adj_final.shape[3]
    slots = proj_blocks.shape[3]
    group = lax.axis_size("gy") * lax.axis_size("gz")
    capacity = max(2, (2 * slots + group - 1) // group)
    target = owner_device_index[0, :, 0]
    order = jnp.arange(slots)
    earlier_same = (target[:, None] == target[None, :]) & (order[None, :] < order[:, None])
    rank_in = jnp.sum(earlier_same.astype(jnp.int32), axis=1)
    place = target * capacity + rank_in
    placing = (place[:, None] == jnp.arange(group * capacity)[None, :]).astype(jnp.bfloat16)
    extra = jnp.broadcast_to(owner_element_index.astype(jnp.float32), (8, slots))

    begin = adj_final[0]
    adj_new = reverse_step(new_states[0], begin, get_faces(begin))

    m_tiles = 8 // CHUNKS
    incoming = []
    for chunk in range(CHUNKS):
        outgoing = project(adj_new, proj_blocks, placing, extra, chunk, m_tiles)
        incoming.append(send_to_owners(outgoing, group, capacity))
    adj_proj, *faces = receive(incoming, columns, m_tiles)
    adj_old = reverse_step(old_states[0], adj_proj, faces)
    return (adj_new.reshape(adj_final.shape), adj_old.reshape(adj_final.shape))


def solution(mesh):
    in_specs = (
        P("gx", None, None, ("gy", "gz")),
        P("gx", None, None, None, ("gy", "gz")),
        P("gx", None, None, None, ("gy", "gz")),
        P("gx", ("gy", "gz"), None),
        P("gx", ("gy", "gz")),
        P("gx", None, None, ("gy", "gz")),
    )
    out_specs = (P("gx", None, None, ("gy", "gz")), P("gx", None, None, ("gy", "gz")))
    return jax.shard_map(
        per_device, mesh=mesh, in_specs=in_specs, out_specs=out_specs, check_vma=False
    )
```

```python
import functools

import jax
import jax.numpy as jnp
import numpy as np
from jax import lax
from jax.experimental import pallas as pl
from jax.experimental.pallas import tpu as pltpu
from jax.sharding import PartitionSpec as P

ELEMENTS_Z = 64

step_rate = 0.01
lift_scale = 6.0
half_lift = 3.0
vmem_limit = 40 * 1024 * 1024
VARS = 5
LANES = 128


def swapped(value, axis, offset):
    count = lax.axis_size(axis)
    pairs = []
    for source in range(count):
        up = source % 2 == offset
        pairs.append((source, (source + (1 if up else -1)) % count))
    return lax.ppermute(value, axis, pairs)


def even_places():
    along_x = lax.axis_index("gx")
    along_y = lax.axis_index("gy") * lax.axis_size("gz") + lax.axis_index("gz")
    return lax.rem(along_x, 2) == 0, lax.rem(along_y, 2) == 0


def lgl_matrix():
    points = np.array([-1.0, -1.0 / np.sqrt(5.0), 1.0 / np.sqrt(5.0), 1.0])
    factors = np.array(
        [np.prod([points[i] - points[j] for j in range(4) if j != i]) for i in range(4)]
    )
    deriv_table = np.zeros((4, 4))
    for i in range(4):
        for j in range(4):
            if i != j:
                deriv_table[i, j] = factors[i] / (factors[j] * (points[i] - points[j]))
    for i in range(4):
        deriv_table[i, i] = -np.sum(deriv_table[i])
    return deriv_table


face_table = lgl_matrix()
face_table[0, 0] += half_lift
face_table[3, 3] -= half_lift
assert np.max(np.abs(np.diag(face_table))) < 1e-12


def iotas():
    row = lax.broadcasted_iota(jnp.int32, (8, LANES), 0)
    lane = lax.broadcasted_iota(jnp.int32, (8, LANES), 1)
    return row, lane


def by_sublane(row, values):
    out = jnp.full((8, LANES), np.float32(values[7]))
    for s in range(6, -1, -1):
        out = jnp.where(row == s, np.float32(values[s]), out)
    return out


def tile_of(ref, v, i, j):
    lead = v if isinstance(v, tuple) else (v,)
    return ref[lead + (slice(8 * i, 8 * i + 8), slice(LANES * j, LANES * (j + 1)))]


def primitive_state(get):
    inverse = 1.0 / get(0)
    speeds = [get(1 + d) * inverse for d in range(3)]
    kinetic = (
        get(1) * speeds[0] + get(2) * speeds[1] + get(3) * speeds[2]
    )
    energy = get(4)
    pressure = 0.4 * (energy - 0.5 * kinetic)
    return speeds, (energy + pressure) * inverse


def pull_full(speeds, enthalpy, v):
    total = v[0][4] * speeds[0] + v[1][4] * speeds[1] + v[2][4] * speeds[2]
    weight = v[0][1] + v[1][2] + v[2][3] + total
    fifth = 0.2 * weight
    pulled = []
    for d in range(3):
        part = (
            v[d][1] * speeds[0]
            + v[d][2] * speeds[1]
            + v[d][3] * speeds[2]
            + v[d][4] * enthalpy
        )
        pulled.append(part - fifth * speeds[d])
    out = [-(pulled[0] * speeds[0] + pulled[1] * speeds[1] + pulled[2] * speeds[2])]
    for j in range(3):
        moved = (
            v[0][1 + j] * speeds[0] + v[1][1 + j] * speeds[1] + v[2][1 + j] * speeds[2]
        )
        out.append(v[j][0] + moved - fifth * speeds[j] + pulled[j])
    out.append(total + 2.0 * fifth)
    return out


def pull_one(direction, speeds, enthalpy, v):
    own = speeds[direction]
    total = v[4] * own
    fifth = 0.2 * (v[1 + direction] + total)
    pulled = [-fifth * speeds[d] for d in range(3)]
    pulled[direction] = (
        v[1] * speeds[0]
        + v[2] * speeds[1]
        + v[3] * speeds[2]
        + v[4] * enthalpy
        + pulled[direction]
    )
    out = [-(pulled[0] * speeds[0] + pulled[1] * speeds[1] + pulled[2] * speeds[2])]
    for j in range(3):
        moved = v[1 + j] * own - fifth * speeds[j] + pulled[j]
        out.append(v[0] + moved if j == direction else moved)
    out.append(total + 2.0 * fifth)
    return out


def local_kernel(scale, index, extras, halves, *refs):
    state_ref, w_ref = refs[0], refs[1]
    extra_refs = refs[2 : 2 + len(extras)]
    out_ref = refs[2 + len(extras)]
    row, lane = iotas()
    low_half_rows = row < 4
    low_half_lanes = lane < 64
    z_first = lane % ELEMENTS_Z == 0
    z_last = lane % ELEMENTS_Z == ELEMENTS_Z - 1
    z_shift = {}
    for k in (1, 2, 3, -1, -2, -3):
        column = [
            face_table[s % 4 - k, s % 4] if 0 <= s % 4 - k <= 3 else 0.0 for s in range(8)
        ]
        z_shift[k] = by_sublane(row, column)
    z_low = by_sublane(row, [half_lift if s % 4 == 0 else 0.0 for s in range(8)])
    z_high = by_sublane(row, [-half_lift if s % 4 == 3 else 0.0 for s in range(8)])
    zero = jnp.zeros((8, LANES), jnp.float32)

    for j in range(halves):
        for i in range(8):
            a, t = i // 2, i % 2
            other = 2 * a + 1 - t
            bs = [2 * t + s // 4 for s in range(8)]
            y_same = by_sublane(row, [face_table[2 * (1 - t) + s // 4, bs[s]] for s in range(8)])
            y_swap = by_sublane(row, [face_table[2 * t + 1 - s // 4, bs[s]] for s in range(8)])
            y_both = by_sublane(
                row, [face_table[2 * (1 - t) + 1 - s // 4, bs[s]] for s in range(8)]
            )
            y_face_rows = low_half_rows if t == 0 else jnp.logical_not(low_half_rows)
            y_sign = half_lift if t == 0 else -half_lift
            y_face = jnp.where(y_face_rows, np.float32(y_sign), 0.0)
            count = by_sublane(
                row,
                [
                    lift_scale
                    * ((a in (0, 3)) + (bs[s] in (0, 3)) + (s % 4 in (0, 3)))
                    for s in range(8)
                ],
            )
            v = [[], [], []]
            penalties = []
            for var in range(VARS):
                w = tile_of(w_ref, var, i, j)
                acc = None
                for source in range(4):
                    if source == a:
                        continue
                    term = np.float32(face_table[source, a]) * tile_of(
                        w_ref, var, 2 * source + t, j
                    )
                    acc = term if acc is None else acc + term
                v[0].append(acc)
                pair = tile_of(w_ref, var, other, j)
                pair_swapped = pltpu.roll(pair, 4, 0)
                acc = (
                    y_same * pair
                    + y_swap * pltpu.roll(w, 4, 0)
                    + y_both * pair_swapped
                )
                here = pltpu.roll(pair_swapped, 64, 1)
                if t == 0:
                    before = (
                        pltpu.roll(pltpu.roll(tile_of(w_ref, var, other, j - 1), 4, 0), 64, 1)
                        if j > 0
                        else zero
                    )
                    y_in = jnp.where(low_half_lanes, before, here)
                else:
                    after = (
                        pltpu.roll(pltpu.roll(tile_of(w_ref, var, other, j + 1), 4, 0), 64, 1)
                        if j < halves - 1
                        else zero
                    )
                    y_in = jnp.where(low_half_lanes, here, after)
                y_term = y_face * y_in
                v[1].append(acc + y_term)
                acc = None
                moved = {}
                for k in (1, 2, 3, -1, -2, -3):
                    moved[k] = pltpu.roll(w, k % 8, 0)
                    term = z_shift[k] * moved[k]
                    acc = term if acc is None else acc + term
                below = jnp.where(
                    z_first, pltpu.roll(moved[-3], 65, 1), pltpu.roll(moved[-3], 1, 1)
                )
                above = jnp.where(
                    z_last, pltpu.roll(moved[3], 63, 1), pltpu.roll(moved[3], 127, 1)
                )
                low_term = z_low * below
                high_term = z_high * above
                v[2].append(acc + low_term + high_term)
                y_jump = y_term if t == 0 else -y_term
                penalties.append(
                    count * w - 2.0 * (y_jump + (low_term - high_term))
                )
            speeds, enthalpy = primitive_state(lambda q: tile_of(state_ref, (index, q), i, j))
            pulled = pull_full(speeds, enthalpy, v)
            for var in range(VARS):
                change = (-step_rate * scale) * (pulled[var] + penalties[var])
                base = scale * tile_of(w_ref, var, i, j)
                for ref, factor in zip(extra_refs, extras):
                    base = base + np.float32(factor) * tile_of(ref, var, i, j)
                out_ref[var, 8 * i : 8 * i + 8, LANES * j : LANES * (j + 1)] = base + change


def pack_faces(w_ref, halves, xa_ref, xb_ref, ya_ref, yb_ref):
    even_x, even_y = even_places()
    row, lane = iotas()
    low_rows = row < 4
    low_lanes = lane < 64
    for var in range(VARS):
        lower = w_ref[var, 0:16, :]
        upper = w_ref[var, 48:64, :]
        xa_ref[var] = jnp.where(even_x, upper, lower)
        xb_ref[var] = jnp.where(even_x, lower, upper)
        low = [tile_of(w_ref, var, 2 * a, 0) for a in range(4)]
        left = jnp.where(low_rows, low[0], pltpu.roll(low[1], 4, 0))
        right = jnp.where(low_rows, low[2], pltpu.roll(low[3], 4, 0))
        lower = jnp.where(low_lanes, left, pltpu.roll(right, 64, 1))
        high = [tile_of(w_ref, var, 2 * a + 1, halves - 1) for a in range(4)]
        left = jnp.where(low_rows, pltpu.roll(high[0], 4, 0), high[1])
        right = jnp.where(low_rows, pltpu.roll(high[2], 4, 0), high[3])
        upper = jnp.where(low_lanes, pltpu.roll(left, 64, 1), right)
        ya_ref[var] = jnp.where(even_y, upper, lower)
        yb_ref[var] = jnp.where(even_y, lower, upper)


def face_kernel(halves, w_ref, *out_refs):
    pack_faces(w_ref, halves, *out_refs)


def finish_kernel(
    scale, index, with_faces, halves, state_ref, base_ref, xa_ref, xb_ref, ya_ref, yb_ref, *outs
):
    out_ref = outs[0]
    even_x, even_y = even_places()
    row, lane = iotas()
    rate = np.float32(-step_rate * scale)
    y_low_mask = jnp.where(jnp.logical_and(row < 4, lane < 64), np.float32(half_lift), 0.0)
    y_high_mask = jnp.where(jnp.logical_and(row >= 4, lane >= 64), np.float32(-half_lift), 0.0)
    for j in range(halves):
        for i in range(8):
            a, t = i // 2, i % 2
            has_x = a in (0, 3)
            has_y = (t == 0 and j == 0) or (t == 1 and j == halves - 1)
            place = (slice(8 * i, 8 * i + 8), slice(LANES * j, LANES * (j + 1)))
            values = [base_ref[(var,) + place] for var in range(VARS)]
            if has_x or has_y:
                speeds, enthalpy = primitive_state(lambda q: tile_of(state_ref, (index, q), i, j))
            if has_x:
                first = jnp.logical_not(even_x) if a == 0 else even_x
                sign = half_lift if a == 0 else -half_lift
                got = [
                    np.float32(sign)
                    * jnp.where(first, tile_of(xa_ref, var, t, j), tile_of(xb_ref, var, t, j))
                    for var in range(VARS)
                ]
                pulled = pull_one(0, speeds, enthalpy, got)
                jump = 2.0 if a == 0 else -2.0
                values = [
                    x + rate * (g - jump * q) for x, g, q in zip(values, pulled, got)
                ]
            if has_y:
                got = []
                for var in range(VARS):
                    first = jnp.logical_not(even_y) if t == 0 else even_y
                    packed = jnp.where(first, ya_ref[var], yb_ref[var])
                    if t == 0:
                        if a >= 2:
                            packed = pltpu.roll(packed, 64, 1)
                        if a % 2 == 1:
                            packed = pltpu.roll(packed, 4, 0)
                        got.append(y_low_mask * packed)
                    else:
                        if a < 2:
                            packed = pltpu.roll(packed, 64, 1)
                        if a % 2 == 0:
                            packed = pltpu.roll(packed, 4, 0)
                        got.append(y_high_mask * packed)
                pulled = pull_one(1, speeds, enthalpy, got)
                jump = 2.0 if t == 0 else -2.0
                values = [
                    x + rate * (g - jump * q) for x, g, q in zip(values, pulled, got)
                ]
            for var in range(VARS):
                out_ref[(var,) + place] = values[var]
    if with_faces:
        pack_faces(out_ref, halves, *outs[1:])


def vmem_spec():
    return pl.BlockSpec(memory_space=pltpu.VMEM)


def params():
    return pltpu.CompilerParams(vmem_limit_bytes=vmem_limit)


def face_shapes(columns):
    return [
        jax.ShapeDtypeStruct((VARS, 16, columns), jnp.float32),
        jax.ShapeDtypeStruct((VARS, 16, columns), jnp.float32),
        jax.ShapeDtypeStruct((VARS, 8, LANES), jnp.float32),
        jax.ShapeDtypeStruct((VARS, 8, LANES), jnp.float32),
    ]


def get_faces(w):
    columns = w.shape[2]
    return pl.pallas_call(
        functools.partial(face_kernel, columns // LANES),
        out_shape=face_shapes(columns),
        in_specs=[vmem_spec()],
        out_specs=[vmem_spec()] * 4,
        compiler_params=params(),
        name="faces",
    )(w)


def exchange(faces):
    xa, xb, ya, yb = faces
    ring = ("gy", "gz")
    xb = swapped(xb, "gx", 1)
    xa = swapped(xa, "gx", 0)
    yb = swapped(yb, ring, 1)
    ya = swapped(ya, ring, 0)
    return xa, xb, ya, yb


def section(states, index, w, faces, scale, extras, with_faces):
    columns = w.shape[2]
    halves = columns // LANES
    shape = jax.ShapeDtypeStruct(w.shape, jnp.float32)
    received = exchange(faces)
    factors = tuple(f for _, f in extras)
    base = pl.pallas_call(
        functools.partial(local_kernel, scale, index, factors, halves),
        out_shape=shape,
        in_specs=[vmem_spec()] * (2 + len(extras)),
        out_specs=vmem_spec(),
        compiler_params=params(),
        cost_estimate=pl.CostEstimate(
            flops=400 * 64 * columns, bytes_accessed=12 * VARS * 64 * columns, transcendentals=0
        ),
        name="local_part",
    )(states, w, *[x for x, _ in extras])
    out_shape = [shape] + (face_shapes(columns) if with_faces else [])
    return pl.pallas_call(
        functools.partial(finish_kernel, scale, index, with_faces, halves),
        out_shape=out_shape,
        in_specs=[vmem_spec()] * 6,
        out_specs=[vmem_spec()] * len(out_shape),
        compiler_params=params(),
        name="finish",
    )(states, base, *received)


def reverse_step(states, begin, faces):
    second, *faces = section(states, 2, begin, faces, 2.0 / 3.0, [], True)
    first, *faces = section(states, 1, second, faces, 0.25, [], True)
    (result,) = section(
        states, 0, first, faces, 1.0, [(begin, 1.0 / 3.0), (second, 0.75)], False
    )
    return result


def split_three(x):
    high = x.astype(jnp.bfloat16)
    rest = x - high.astype(jnp.float32)
    middle = rest.astype(jnp.bfloat16)
    low = (rest - middle.astype(jnp.float32)).astype(jnp.bfloat16)
    return high, middle, low


def project_kernel(first, m_tiles, blocks, with_copy, *refs):
    w_ref, block_ref, placing_ref, extra_ref = refs[:4]
    out_refs = refs[4 : 4 + blocks]
    held = refs[-2]
    if with_copy:
        copy = pltpu.make_async_copy(w_ref, refs[4 + blocks], refs[-1].at[0])
        copy.start()
    halves = w_ref.shape[2] // LANES
    for r in range(block_ref.shape[3] // LANES):
        lanes = slice(LANES * r, LANES * (r + 1))
        half = r % halves
        w_lanes = slice(LANES * half, LANES * (half + 1))

        def body(tile, sums):
            start = pl.multiple_of(8 * tile, 8)
            groups = [w_ref[var, pl.ds(start, 8), w_lanes] for var in range(VARS)]
            sums = list(sums)
            for s in range(8):
                rows = [jnp.broadcast_to(group[s : s + 1], (8, LANES)) for group in groups]
                for m in range(m_tiles):
                    node = 8 * (first + m)
                    block = block_ref[0, start + s, node : node + 8, lanes]
                    for var in range(VARS):
                        q = m * VARS + var
                        sums[q] = sums[q] + block * rows[var]
            return tuple(sums)

        start = tuple(jnp.zeros((8, LANES), jnp.float32) for _ in range(m_tiles * VARS))
        sums = lax.fori_loop(0, 8, body, start)
        for q in range(m_tiles * VARS):
            held[8 * q : 8 * q + 8, lanes] = sums[q]

    values = jnp.concatenate([held[...], extra_ref[...]], axis=0)
    total = values.shape[0]
    pieces = jnp.concatenate(split_three(values), axis=0)
    result = jnp.dot(pieces, placing_ref[...], preferred_element_type=jnp.float32)
    result = result[0:total] + result[total : 2 * total] + result[2 * total :]
    for g in range(blocks):
        out_refs[g][...] = result[:, LANES * g : LANES * (g + 1)]
    if with_copy:
        copy.wait()


def project(w, blocks, placing, extra, first, m_tiles, with_copy):
    slots = blocks.shape[3]
    rows = m_tiles * VARS * 8
    count = placing.shape[1] // LANES
    out_shape = [jax.ShapeDtypeStruct((rows + 8, LANES), jnp.float32)] * count
    out_specs = [vmem_spec()] * count
    if with_copy:
        out_shape.append(jax.ShapeDtypeStruct(w.shape, jnp.float32))
        out_specs.append(pl.BlockSpec(memory_space=pl.ANY))
    return pl.pallas_call(
        functools.partial(project_kernel, first * m_tiles, m_tiles, count, with_copy),
        out_shape=out_shape,
        in_specs=[vmem_spec()] * 4,
        out_specs=out_specs,
        scratch_shapes=[
            pltpu.VMEM((rows, slots), jnp.float32),
            pltpu.SemaphoreType.DMA((1,)),
        ],
        compiler_params=params(),
        cost_estimate=pl.CostEstimate(
            flops=5 * 1000 * 1000 * 1000,
            bytes_accessed=4 * rows * 64 * slots,
            transcendentals=0,
        ),
        name="project",
    )(w, blocks, placing, extra)


def receive_kernel(blocks, node, m_tiles, last, halves, *refs):
    out_ref = refs[blocks + (1 if last else 0)]
    columns = out_ref.shape[2]
    rows = m_tiles * VARS * 8
    if last:
        done_ref = refs[blocks]
        for var in range(VARS):
            out_ref[var, 0:node, :] = done_ref[var]
    result = jnp.zeros((rows, columns), jnp.float32)
    for g in range(blocks):
        local = refs[g][rows : rows + 1, :].astype(jnp.int32)
        index = lax.broadcasted_iota(jnp.int32, (columns, LANES), 0)
        spot = (index == local).astype(jnp.float32).astype(jnp.bfloat16)
        for piece in split_three(refs[g][0:rows, :]):
            result = result + lax.dot_general(
                piece, spot, (((1,), (1,)), ((), ())), preferred_element_type=jnp.float32
            )
    base = node if last else 0
    for m in range(m_tiles):
        for var in range(VARS):
            q = m * VARS + var
            out_ref[var, base + 8 * m : base + 8 * m + 8, :] = result[8 * q : 8 * q + 8, :]
    if last:
        pack_faces(out_ref, halves, *refs[blocks + 2 :])


def receive(incoming, columns, node, m_tiles, done):
    last = done is not None
    if last:
        shapes = [jax.ShapeDtypeStruct((VARS, 64, columns), jnp.float32)] + face_shapes(columns)
    else:
        shapes = [jax.ShapeDtypeStruct((VARS, 8 * m_tiles, columns), jnp.float32)]
    operands = list(incoming) + ([done] if last else [])
    return pl.pallas_call(
        functools.partial(
            receive_kernel, len(incoming), node, m_tiles, last, columns // LANES
        ),
        out_shape=shapes,
        in_specs=[vmem_spec()] * len(operands),
        out_specs=[vmem_spec()] * len(shapes),
        compiler_params=params(),
        cost_estimate=pl.CostEstimate(
            flops=1000 * 1000 * 1000, bytes_accessed=1000 * 1000, transcendentals=0
        ),
        name="receive",
    )(*operands)


def send_direct(values):
    ring = ("gy", "gz")
    count = len(values)
    received = [values[0]] * count
    for k in (6, 7, 2, 4, 3, 5, 1):
        if k < count:
            received[k] = lax.ppermute(values[k], ring, [(s, s ^ k) for s in range(count)])
    return received


def send_all(values, group, capacity):
    values = jnp.stack(values)
    blocks, rows, lanes = values.shape
    per = lanes // capacity
    values = values.reshape(blocks, rows, per, capacity).transpose(0, 2, 1, 3)
    values = values.reshape(group, rows, capacity)
    values = lax.all_to_all(values, ("gy", "gz"), split_axis=0, concat_axis=0, tiled=True)
    values = values.reshape(blocks, per, rows, capacity).transpose(0, 2, 1, 3)
    values = values.reshape(blocks, rows, lanes)
    return [values[g] for g in range(blocks)]


CHUNKS = 2


def per_device(
    adj_final, new_states, old_states, owner_device_index, owner_element_index, proj_blocks
):
    columns = adj_final.shape[3]
    slots = proj_blocks.shape[3]
    group = lax.axis_size("gy") * lax.axis_size("gz")
    capacity = max(2, (2 * slots + group - 1) // group)
    target = owner_device_index[0, :, 0]
    order = jnp.arange(slots)
    earlier_same = (target[:, None] == target[None, :]) & (order[None, :] < order[:, None])
    rank_in = jnp.sum(earlier_same.astype(jnp.int32), axis=1)
    direct = group in (2, 4, 8) and capacity == LANES
    if direct:
        here = lax.axis_index("gy") * lax.axis_size("gz") + lax.axis_index("gz")
        target = jnp.bitwise_xor(target, here)
    place = target * capacity + rank_in
    placing = (place[:, None] == jnp.arange(group * capacity)[None, :]).astype(jnp.bfloat16)
    extra = jnp.broadcast_to(owner_element_index.astype(jnp.float32), (8, slots))

    begin = adj_final[0]
    result = reverse_step(new_states[0], begin, get_faces(begin))

    m_tiles = 8 // CHUNKS
    incoming = []
    for chunk in range(CHUNKS):
        last = chunk == CHUNKS - 1
        outgoing = project(result, proj_blocks, placing, extra, chunk, m_tiles, last)
        if last:
            adj_new = outgoing[-1]
            outgoing = outgoing[:-1]
        incoming.append(
            send_direct(outgoing) if direct else send_all(outgoing, group, capacity)
        )
    (half,) = receive(incoming[0], columns, 0, m_tiles, None)
    adj_proj, *faces = receive(incoming[1], columns, 8 * m_tiles, m_tiles, half)
    adj_old = reverse_step(old_states[0], adj_proj, faces)
    return (adj_new.reshape(adj_final.shape), adj_old.reshape(adj_final.shape))


def solution(mesh):
    in_specs = (
        P("gx", None, None, ("gy", "gz")),
        P("gx", None, None, None, ("gy", "gz")),
        P("gx", None, None, None, ("gy", "gz")),
        P("gx", ("gy", "gz"), None),
        P("gx", ("gy", "gz")),
        P("gx", None, None, ("gy", "gz")),
    )
    out_specs = (P("gx", None, None, ("gy", "gz")), P("gx", None, None, ("gy", "gz")))
    return jax.shard_map(
        per_device, mesh=mesh, in_specs=in_specs, out_specs=out_specs, check_vma=False
    )
```

```python
import functools

import jax
import jax.numpy as jnp
import numpy as np
from jax import lax
from jax.experimental import pallas as pl
from jax.experimental.pallas import tpu as pltpu
from jax.sharding import PartitionSpec as P

ELEMENTS_Z = 64

step_rate = 0.01
lift_scale = 6.0
half_lift = 3.0
vmem_limit = 24 * 1024 * 1024
VARS = 5
LANES = 128


def swapped(value, axis, offset):
    count = lax.axis_size(axis)
    pairs = []
    for source in range(count):
        up = source % 2 == offset
        pairs.append((source, (source + (1 if up else -1)) % count))
    return lax.ppermute(value, axis, pairs)


def even_places():
    along_x = lax.axis_index("gx")
    along_y = lax.axis_index("gy") * lax.axis_size("gz") + lax.axis_index("gz")
    return lax.rem(along_x, 2) == 0, lax.rem(along_y, 2) == 0


def lgl_matrix():
    points = np.array([-1.0, -1.0 / np.sqrt(5.0), 1.0 / np.sqrt(5.0), 1.0])
    factors = np.array(
        [np.prod([points[i] - points[j] for j in range(4) if j != i]) for i in range(4)]
    )
    deriv_table = np.zeros((4, 4))
    for i in range(4):
        for j in range(4):
            if i != j:
                deriv_table[i, j] = factors[i] / (factors[j] * (points[i] - points[j]))
    for i in range(4):
        deriv_table[i, i] = -np.sum(deriv_table[i])
    return deriv_table


face_table = lgl_matrix()
face_table[0, 0] += half_lift
face_table[3, 3] -= half_lift
assert np.max(np.abs(np.diag(face_table))) < 1e-12


def iotas():
    row = lax.broadcasted_iota(jnp.int32, (8, LANES), 0)
    lane = lax.broadcasted_iota(jnp.int32, (8, LANES), 1)
    return row, lane


def by_sublane(row, values):
    out = jnp.full((8, LANES), np.float32(values[7]))
    for s in range(6, -1, -1):
        out = jnp.where(row == s, np.float32(values[s]), out)
    return out


def tile_of(ref, v, i, j):
    lead = v if isinstance(v, tuple) else (v,)
    return ref[lead + (slice(8 * i, 8 * i + 8), slice(LANES * j, LANES * (j + 1)))]


def primitive_state(get):
    inverse = 1.0 / get(0)
    speeds = [get(1 + d) * inverse for d in range(3)]
    kinetic = (
        get(1) * speeds[0] + get(2) * speeds[1] + get(3) * speeds[2]
    )
    energy = get(4)
    pressure = 0.4 * (energy - 0.5 * kinetic)
    return speeds, (energy + pressure) * inverse


def pull_full(speeds, enthalpy, v):
    total = v[0][4] * speeds[0] + v[1][4] * speeds[1] + v[2][4] * speeds[2]
    weight = v[0][1] + v[1][2] + v[2][3] + total
    fifth = 0.2 * weight
    pulled = []
    for d in range(3):
        part = (
            v[d][1] * speeds[0]
            + v[d][2] * speeds[1]
            + v[d][3] * speeds[2]
            + v[d][4] * enthalpy
        )
        pulled.append(part - fifth * speeds[d])
    out = [-(pulled[0] * speeds[0] + pulled[1] * speeds[1] + pulled[2] * speeds[2])]
    for j in range(3):
        moved = (
            v[0][1 + j] * speeds[0] + v[1][1 + j] * speeds[1] + v[2][1 + j] * speeds[2]
        )
        out.append(v[j][0] + moved - fifth * speeds[j] + pulled[j])
    out.append(total + 2.0 * fifth)
    return out


def pull_one(direction, speeds, enthalpy, v):
    own = speeds[direction]
    total = v[4] * own
    fifth = 0.2 * (v[1 + direction] + total)
    pulled = [-fifth * speeds[d] for d in range(3)]
    pulled[direction] = (
        v[1] * speeds[0]
        + v[2] * speeds[1]
        + v[3] * speeds[2]
        + v[4] * enthalpy
        + pulled[direction]
    )
    out = [-(pulled[0] * speeds[0] + pulled[1] * speeds[1] + pulled[2] * speeds[2])]
    for j in range(3):
        moved = v[1 + j] * own - fifth * speeds[j] + pulled[j]
        out.append(v[0] + moved if j == direction else moved)
    out.append(total + 2.0 * fifth)
    return out


def local_kernel(scale, index, extras, halves, *refs):
    state_ref, w_ref = refs[0], refs[1]
    extra_refs = refs[2 : 2 + len(extras)]
    out_ref = refs[2 + len(extras)]
    row, lane = iotas()
    low_half_rows = row < 4
    low_half_lanes = lane < 64
    z_first = lane % ELEMENTS_Z == 0
    z_last = lane % ELEMENTS_Z == ELEMENTS_Z - 1
    z_shift = {}
    for k in (1, 2, 3, -1, -2, -3):
        column = [
            face_table[s % 4 - k, s % 4] if 0 <= s % 4 - k <= 3 else 0.0 for s in range(8)
        ]
        z_shift[k] = by_sublane(row, column)
    z_low = by_sublane(row, [half_lift if s % 4 == 0 else 0.0 for s in range(8)])
    z_high = by_sublane(row, [-half_lift if s % 4 == 3 else 0.0 for s in range(8)])
    zero = jnp.zeros((8, LANES), jnp.float32)

    for j in range(halves):
        for i in range(8):
            a, t = i // 2, i % 2
            other = 2 * a + 1 - t
            bs = [2 * t + s // 4 for s in range(8)]
            y_same = by_sublane(row, [face_table[2 * (1 - t) + s // 4, bs[s]] for s in range(8)])
            y_swap = by_sublane(row, [face_table[2 * t + 1 - s // 4, bs[s]] for s in range(8)])
            y_both = by_sublane(
                row, [face_table[2 * (1 - t) + 1 - s // 4, bs[s]] for s in range(8)]
            )
            y_face_rows = low_half_rows if t == 0 else jnp.logical_not(low_half_rows)
            y_sign = half_lift if t == 0 else -half_lift
            y_face = jnp.where(y_face_rows, np.float32(y_sign), 0.0)
            count = by_sublane(
                row,
                [
                    lift_scale
                    * ((a in (0, 3)) + (bs[s] in (0, 3)) + (s % 4 in (0, 3)))
                    for s in range(8)
                ],
            )
            v = [[], [], []]
            penalties = []
            for var in range(VARS):
                w = tile_of(w_ref, var, i, j)
                acc = None
                for source in range(4):
                    if source == a:
                        continue
                    term = np.float32(face_table[source, a]) * tile_of(
                        w_ref, var, 2 * source + t, j
                    )
                    acc = term if acc is None else acc + term
                v[0].append(acc)
                pair = tile_of(w_ref, var, other, j)
                pair_swapped = pltpu.roll(pair, 4, 0)
                acc = (
                    y_same * pair
                    + y_swap * pltpu.roll(w, 4, 0)
                    + y_both * pair_swapped
                )
                here = pltpu.roll(pair_swapped, 64, 1)
                if t == 0:
                    before = (
                        pltpu.roll(pltpu.roll(tile_of(w_ref, var, other, j - 1), 4, 0), 64, 1)
                        if j > 0
                        else zero
                    )
                    y_in = jnp.where(low_half_lanes, before, here)
                else:
                    after = (
                        pltpu.roll(pltpu.roll(tile_of(w_ref, var, other, j + 1), 4, 0), 64, 1)
                        if j < halves - 1
                        else zero
                    )
                    y_in = jnp.where(low_half_lanes, here, after)
                y_term = y_face * y_in
                v[1].append(acc + y_term)
                acc = None
                moved = {}
                for k in (1, 2, 3, -1, -2, -3):
                    moved[k] = pltpu.roll(w, k % 8, 0)
                    term = z_shift[k] * moved[k]
                    acc = term if acc is None else acc + term
                below = jnp.where(
                    z_first, pltpu.roll(moved[-3], 65, 1), pltpu.roll(moved[-3], 1, 1)
                )
                above = jnp.where(
                    z_last, pltpu.roll(moved[3], 63, 1), pltpu.roll(moved[3], 127, 1)
                )
                low_term = z_low * below
                high_term = z_high * above
                v[2].append(acc + low_term + high_term)
                y_jump = y_term if t == 0 else -y_term
                penalties.append(
                    count * w - 2.0 * (y_jump + (low_term - high_term))
                )
            speeds, enthalpy = primitive_state(lambda q: tile_of(state_ref, (index, q), i, j))
            pulled = pull_full(speeds, enthalpy, v)
            for var in range(VARS):
                change = (-step_rate * scale) * (pulled[var] + penalties[var])
                base = scale * tile_of(w_ref, var, i, j)
                for ref, factor in zip(extra_refs, extras):
                    base = base + np.float32(factor) * tile_of(ref, var, i, j)
                out_ref[var, 8 * i : 8 * i + 8, LANES * j : LANES * (j + 1)] = base + change


def pack_x(lower, upper, xa_ref, xb_ref):
    even_x, _ = even_places()
    for var in range(VARS):
        xa_ref[var] = jnp.where(even_x, upper[var], lower[var])
        xb_ref[var] = jnp.where(even_x, lower[var], upper[var])


def pack_y(low_of, high_of, ya_ref, yb_ref):
    _, even_y = even_places()
    row, lane = iotas()
    low_rows = row < 4
    low_lanes = lane < 64
    for var in range(VARS):
        low = [low_of(var, a) for a in range(4)]
        left = jnp.where(low_rows, low[0], pltpu.roll(low[1], 4, 0))
        right = jnp.where(low_rows, low[2], pltpu.roll(low[3], 4, 0))
        lower = jnp.where(low_lanes, left, pltpu.roll(right, 64, 1))
        high = [high_of(var, a) for a in range(4)]
        left = jnp.where(low_rows, pltpu.roll(high[0], 4, 0), high[1])
        right = jnp.where(low_rows, pltpu.roll(high[2], 4, 0), high[3])
        upper = jnp.where(low_lanes, pltpu.roll(left, 64, 1), right)
        ya_ref[var] = jnp.where(even_y, upper, lower)
        yb_ref[var] = jnp.where(even_y, lower, upper)


def pack_faces(w_ref, halves, xa_ref, xb_ref, ya_ref, yb_ref):
    lower = [w_ref[var, 0:16, :] for var in range(VARS)]
    upper = [w_ref[var, 48:64, :] for var in range(VARS)]
    pack_x(lower, upper, xa_ref, xb_ref)
    pack_y(
        lambda var, a: tile_of(w_ref, var, 2 * a, 0),
        lambda var, a: tile_of(w_ref, var, 2 * a + 1, halves - 1),
        ya_ref,
        yb_ref,
    )


def face_kernel(halves, w_hbm, state_hbm, w_ref, state_ref, *refs):
    sems = refs[-1]
    first = pltpu.make_async_copy(w_hbm.at[0], w_ref, sems.at[0])
    second = pltpu.make_async_copy(state_hbm.at[0], state_ref, sems.at[1])
    first.start()
    second.start()
    first.wait()
    pack_faces(w_ref, halves, *refs[:-1])
    second.wait()


def finish_kernel(
    scale, index, with_faces, halves, state_ref, base_ref, xa_ref, xb_ref, ya_ref, yb_ref, *outs
):
    out_ref = outs[0]
    even_x, even_y = even_places()
    row, lane = iotas()
    rate = np.float32(-step_rate * scale)
    y_low_mask = jnp.where(jnp.logical_and(row < 4, lane < 64), np.float32(half_lift), 0.0)
    y_high_mask = jnp.where(jnp.logical_and(row >= 4, lane >= 64), np.float32(-half_lift), 0.0)
    for j in range(halves):
        for i in range(8):
            a, t = i // 2, i % 2
            has_x = a in (0, 3)
            has_y = (t == 0 and j == 0) or (t == 1 and j == halves - 1)
            place = (slice(8 * i, 8 * i + 8), slice(LANES * j, LANES * (j + 1)))
            values = [base_ref[(var,) + place] for var in range(VARS)]
            if has_x or has_y:
                speeds, enthalpy = primitive_state(lambda q: tile_of(state_ref, (index, q), i, j))
            if has_x:
                first = jnp.logical_not(even_x) if a == 0 else even_x
                sign = half_lift if a == 0 else -half_lift
                got = [
                    np.float32(sign)
                    * jnp.where(first, tile_of(xa_ref, var, t, j), tile_of(xb_ref, var, t, j))
                    for var in range(VARS)
                ]
                pulled = pull_one(0, speeds, enthalpy, got)
                jump = 2.0 if a == 0 else -2.0
                values = [
                    x + rate * (g - jump * q) for x, g, q in zip(values, pulled, got)
                ]
            if has_y:
                got = []
                for var in range(VARS):
                    first = jnp.logical_not(even_y) if t == 0 else even_y
                    packed = jnp.where(first, ya_ref[var], yb_ref[var])
                    if t == 0:
                        if a >= 2:
                            packed = pltpu.roll(packed, 64, 1)
                        if a % 2 == 1:
                            packed = pltpu.roll(packed, 4, 0)
                        got.append(y_low_mask * packed)
                    else:
                        if a < 2:
                            packed = pltpu.roll(packed, 64, 1)
                        if a % 2 == 0:
                            packed = pltpu.roll(packed, 4, 0)
                        got.append(y_high_mask * packed)
                pulled = pull_one(1, speeds, enthalpy, got)
                jump = 2.0 if t == 0 else -2.0
                values = [
                    x + rate * (g - jump * q) for x, g, q in zip(values, pulled, got)
                ]
            for var in range(VARS):
                out_ref[(var,) + place] = values[var]
    if with_faces:
        pack_faces(out_ref, halves, *outs[1:])


def vmem_spec():
    return pl.BlockSpec(memory_space=pltpu.VMEM)


def params():
    return pltpu.CompilerParams(vmem_limit_bytes=vmem_limit)


def face_shapes(columns):
    return [
        jax.ShapeDtypeStruct((VARS, 16, columns), jnp.float32),
        jax.ShapeDtypeStruct((VARS, 16, columns), jnp.float32),
        jax.ShapeDtypeStruct((VARS, 8, LANES), jnp.float32),
        jax.ShapeDtypeStruct((VARS, 8, LANES), jnp.float32),
    ]


def in_hbm(x):
    return pltpu.with_memory_space_constraint(x, pltpu.HBM)


def hbm_spec():
    return pl.BlockSpec(memory_space=pltpu.HBM)


def get_faces(w, states):
    columns = w.shape[3]
    shapes = [
        jax.ShapeDtypeStruct(w.shape[1:], jnp.float32),
        jax.ShapeDtypeStruct(states.shape[1:], jnp.float32),
    ] + face_shapes(columns)
    begin, states, *faces = pl.pallas_call(
        functools.partial(face_kernel, columns // LANES),
        out_shape=shapes,
        in_specs=[hbm_spec()] * 2,
        out_specs=[vmem_spec()] * len(shapes),
        scratch_shapes=[pltpu.SemaphoreType.DMA((2,))],
        compiler_params=params(),
        name="faces",
    )(in_hbm(w), in_hbm(states))
    return begin, states, faces


def prepare_kernel(spans, group, direct, owner_ref, local_ref, block_ref, after_ref, *refs):
    del after_ref
    out_ref, placing_ref, extra_ref, sems = refs
    copies = []
    at = 0
    for number, (start, size) in enumerate(spans):
        copies.append(
            pltpu.make_async_copy(
                block_ref.at[0, :, start : start + size, :],
                out_ref.at[:, at : at + size, :],
                sems.at[number],
            )
        )
        copies[-1].start()
        at += size
    places, slots = placing_ref.shape
    capacity = places // group
    target = owner_ref[...]
    if direct:
        here = lax.axis_index("gy") * lax.axis_size("gz") + lax.axis_index("gz")
        target = jnp.bitwise_xor(target, here)
    owner = lax.broadcasted_iota(jnp.int32, (group, slots), 0)
    named = jnp.where(owner == target, np.float32(1), np.float32(0))
    earlier = jnp.where(
        lax.broadcasted_iota(jnp.int32, (slots, slots), 0)
        < lax.broadcasted_iota(jnp.int32, (slots, slots), 1),
        np.float32(1),
        np.float32(0),
    )
    ranks = jnp.dot(
        named.astype(jnp.bfloat16),
        earlier.astype(jnp.bfloat16),
        preferred_element_type=jnp.float32,
    )
    rank = jnp.sum(named * ranks, axis=0, keepdims=True).astype(jnp.int32)
    place = target * capacity + rank
    index = lax.broadcasted_iota(jnp.int32, (places, slots), 0)
    placing_ref[...] = jnp.where(index == place, np.float32(1), np.float32(0)).astype(
        jnp.bfloat16
    )
    extra_ref[...] = jnp.broadcast_to(local_ref[...].astype(jnp.float32), extra_ref.shape)
    for copy in copies:
        copy.wait()


def prepare(owners, local, blocks, after, group, capacity, direct):
    slots = blocks.shape[3]
    return pl.pallas_call(
        functools.partial(prepare_kernel, ((0, 16), (48, 16)), group, direct),
        out_shape=[
            jax.ShapeDtypeStruct((64, 32, slots), jnp.float32),
            jax.ShapeDtypeStruct((group * capacity, slots), jnp.bfloat16),
            jax.ShapeDtypeStruct((8, slots), jnp.float32),
        ],
        in_specs=[vmem_spec(), vmem_spec(), hbm_spec(), vmem_spec()],
        out_specs=[vmem_spec()] * 3,
        scratch_shapes=[pltpu.SemaphoreType.DMA((2,))],
        compiler_params=params(),
        name="prepare",
    )(owners, local, in_hbm(blocks), after)


def exchange_x(faces):
    return swapped(faces[1], "gx", 1), swapped(faces[0], "gx", 0)


def exchange_y(faces):
    ring = ("gy", "gz")
    return swapped(faces[1], ring, 1), swapped(faces[0], ring, 0)


def exchange(faces):
    xb, xa = exchange_x(faces[:2])
    yb, ya = exchange_y(faces[2:])
    return xa, xb, ya, yb


def section(states, index, w, received, scale, extras, with_faces):
    columns = w.shape[2]
    halves = columns // LANES
    shape = jax.ShapeDtypeStruct(w.shape, jnp.float32)
    factors = tuple(f for _, f in extras)
    base = pl.pallas_call(
        functools.partial(local_kernel, scale, index, factors, halves),
        out_shape=shape,
        in_specs=[vmem_spec()] * (2 + len(extras)),
        out_specs=vmem_spec(),
        compiler_params=params(),
        cost_estimate=pl.CostEstimate(
            flops=400 * 64 * columns, bytes_accessed=12 * VARS * 64 * columns, transcendentals=0
        ),
        name="local_part",
    )(states, w, *[x for x, _ in extras])
    out_shape = [shape] + (face_shapes(columns) if with_faces else [])
    results = pl.pallas_call(
        functools.partial(finish_kernel, scale, index, with_faces, halves),
        out_shape=out_shape,
        in_specs=[vmem_spec()] * 6,
        out_specs=[vmem_spec()] * len(out_shape),
        compiler_params=params(),
        name="finish",
    )(states, base, *received)
    if with_faces:
        results = [results[0], exchange(results[1:])]
    return results


def reverse_step(states, begin, received):
    second, received = section(states, 2, begin, received, 2.0 / 3.0, [], True)
    first, received = section(states, 1, second, received, 0.25, [], True)
    (result,) = section(
        states, 0, first, received, 1.0, [(begin, 1.0 / 3.0), (second, 0.75)], False
    )
    return result


def split_three(x):
    high = x.astype(jnp.bfloat16)
    rest = x - high.astype(jnp.float32)
    middle = rest.astype(jnp.bfloat16)
    low = (rest - middle.astype(jnp.float32)).astype(jnp.bfloat16)
    return high, middle, low


X_TILES = (0, 1, 6, 7)
REST_TILES = (2, 3, 4, 5)


def project_kernel(tiles, sources, blocks, span, with_copy, *refs):
    w_ref = refs[0]
    block_refs = refs[1 : 1 + sources]
    placing_ref, extra_ref = refs[1 + sources : 3 + sources]
    at = 3 + sources + (1 if span else 0)
    out_refs = refs[at : at + blocks]
    held, sem = refs[-2:]
    if with_copy:
        copy = pltpu.make_async_copy(w_ref, refs[at + blocks], sem.at[0])
        copy.start()
    if span:
        start, size = span
        copy = pltpu.make_async_copy(
            refs[at - 1].at[0, :, start : start + size, :], refs[at + blocks], sem.at[0]
        )
        copy.start()
    halves = w_ref.shape[2] // LANES
    count = len(tiles) * VARS
    for r in range(placing_ref.shape[1] // LANES):
        lanes = slice(LANES * r, LANES * (r + 1))
        half = r % halves
        w_lanes = slice(LANES * half, LANES * (half + 1))

        def body(tile, sums):
            start = pl.multiple_of(8 * tile, 8)
            groups = [w_ref[var, pl.ds(start, 8), w_lanes] for var in range(VARS)]
            sums = list(sums)
            for s in range(8):
                rows = [jnp.broadcast_to(group[s : s + 1], (8, LANES)) for group in groups]
                for m, (source, at) in enumerate(tiles):
                    block = block_refs[source][start + s, 8 * at : 8 * at + 8, lanes]
                    for var in range(VARS):
                        q = m * VARS + var
                        sums[q] = sums[q] + block * rows[var]
            return tuple(sums)

        start = tuple(jnp.zeros((8, LANES), jnp.float32) for _ in range(count))
        sums = lax.fori_loop(0, 8, body, start)
        for q in range(count):
            held[8 * q : 8 * q + 8, lanes] = sums[q]

    values = jnp.concatenate([held[...], extra_ref[...]], axis=0)
    total = values.shape[0]
    pieces = jnp.concatenate(split_three(values), axis=0)
    result = lax.dot_general(
        pieces,
        placing_ref[...],
        (((1,), (1,)), ((), ())),
        preferred_element_type=jnp.float32,
    )
    result = result[0:total] + result[total : 2 * total] + result[2 * total :]
    per = result.shape[1] // blocks
    for g in range(blocks):
        for part in range(per // LANES):
            at = per * g + LANES * part
            out_refs[g][part] = result[:, at : at + LANES]
    if with_copy or span:
        copy.wait()


def project(w, sources, placing, extra, tiles, outputs, load=None, with_copy=False):
    slots = placing.shape[1]
    rows = len(tiles) * VARS * 8
    per = placing.shape[0] // outputs // LANES
    operands = [w, *sources, placing, extra]
    in_specs = [vmem_spec()] * len(operands)
    out_shape = [jax.ShapeDtypeStruct((per, rows + 8, LANES), jnp.float32)] * outputs
    out_specs = [vmem_spec()] * outputs
    span = None
    if load is not None:
        blocks, span = load
        operands.append(in_hbm(blocks))
        in_specs.append(hbm_spec())
        out_shape.append(jax.ShapeDtypeStruct((64, span[1], slots), jnp.float32))
        out_specs.append(vmem_spec())
    if with_copy:
        out_shape.append(jax.ShapeDtypeStruct(w.shape, jnp.float32))
        out_specs.append(pl.BlockSpec(memory_space=pl.ANY))
    results = pl.pallas_call(
        functools.partial(project_kernel, tiles, len(sources), outputs, span, with_copy),
        out_shape=out_shape,
        in_specs=in_specs,
        out_specs=out_specs,
        scratch_shapes=[
            pltpu.VMEM((rows, slots), jnp.float32),
            pltpu.SemaphoreType.DMA((1,)),
        ],
        compiler_params=params(),
        cost_estimate=pl.CostEstimate(
            flops=1000 * 1000 * 1000 * len(tiles),
            bytes_accessed=4 * rows * 64 * slots,
            transcendentals=0,
        ),
        name="project",
    )(*operands)
    return results[:outputs], results[outputs:]


def add_slots(block_refs, firsts, rows, columns):
    result = jnp.zeros((rows, columns), jnp.float32)
    index = lax.broadcasted_iota(jnp.int32, (columns, LANES), 0)
    for number, ref in enumerate(block_refs):
        for g in range(1 if number < firsts else ref.shape[0]):
            local = ref[g, rows : rows + 1, :].astype(jnp.int32)
            spot = (index == local).astype(jnp.float32).astype(jnp.bfloat16)
            for piece in split_three(ref[g, 0:rows, :]):
                result = result + lax.dot_general(
                    piece, spot, (((1,), (1,)), ((), ())), preferred_element_type=jnp.float32
                )
    return result


def receive_x_kernel(count, firsts, *refs):
    out_ref, xa_ref, xb_ref = refs[count:]
    rows, columns = out_ref.shape
    result = add_slots(refs[:count], firsts, rows, columns)
    out_ref[...] = result

    def tile(m, var):
        q = m * VARS + var
        return result[8 * q : 8 * q + 8]

    lower = [jnp.concatenate([tile(0, v), tile(1, v)], axis=0) for v in range(VARS)]
    upper = [jnp.concatenate([tile(2, v), tile(3, v)], axis=0) for v in range(VARS)]
    pack_x(lower, upper, xa_ref, xb_ref)


def receive_rest_kernel(count, firsts, halves, *refs):
    x_ref, out_ref, ya_ref, yb_ref = refs[count:]
    columns = out_ref.shape[2]
    rest = add_slots(refs[:count], firsts, len(REST_TILES) * VARS * 8, columns)
    for var in range(VARS):
        for m, tile in enumerate(X_TILES):
            q = 8 * (m * VARS + var)
            out_ref[var, 8 * tile : 8 * tile + 8, :] = x_ref[q : q + 8, :]
        for m, tile in enumerate(REST_TILES):
            q = 8 * (m * VARS + var)
            out_ref[var, 8 * tile : 8 * tile + 8, :] = rest[q : q + 8]
    pack_y(
        lambda var, a: tile_of(out_ref, var, 2 * a, 0),
        lambda var, a: tile_of(out_ref, var, 2 * a + 1, halves - 1),
        ya_ref,
        yb_ref,
    )


def receive(kernel, operands, shapes, *settings):
    return pl.pallas_call(
        functools.partial(kernel, *settings),
        out_shape=shapes,
        in_specs=[vmem_spec()] * len(operands),
        out_specs=[vmem_spec()] * len(shapes),
        compiler_params=params(),
        cost_estimate=pl.CostEstimate(
            flops=1000 * 1000 * 1000, bytes_accessed=1000 * 1000, transcendentals=0
        ),
        name="receive",
    )(*operands)


def send_chips(values):
    ring = ("gy", "gz")
    count = len(values)
    mine = [values[0]] * count
    for d in range(count - 1, 0, -1):
        pairs = [(s, s ^ (2 * d)) for s in range(2 * count)]
        mine[d] = lax.ppermute(values[d], ring, pairs)
    return mine


def send_cores(mine):
    others = jnp.concatenate([part[1:2] for part in mine], axis=0)
    pairs = [(s, s ^ 1) for s in range(2 * len(mine))]
    return mine + [lax.ppermute(others, ("gy", "gz"), pairs)]


def send_all(values, group, capacity):
    (values,) = values
    blocks, rows, lanes = values.shape
    per = lanes // capacity
    values = values.reshape(blocks, rows, per, capacity).transpose(0, 2, 1, 3)
    values = values.reshape(group, rows, capacity)
    values = lax.all_to_all(values, ("gy", "gz"), split_axis=0, concat_axis=0, tiled=True)
    values = values.reshape(blocks, per, rows, capacity).transpose(0, 2, 1, 3)
    return [values.reshape(blocks, rows, lanes)]


def per_device(
    adj_final, new_states, old_states, owner_device_index, owner_element_index, proj_blocks
):
    columns = adj_final.shape[3]
    slots = proj_blocks.shape[3]
    group = lax.axis_size("gy") * lax.axis_size("gz")
    capacity = max(2, (2 * slots + group - 1) // group)
    begin, states, faces = get_faces(adj_final, new_states)
    received = exchange(faces)
    second, received = section(states, 2, begin, received, 2.0 / 3.0, [], True)

    direct = group in (2, 4, 8) and capacity == LANES
    outputs = group // 2 if direct else 1
    outer, placing, extra = prepare(
        owner_device_index.reshape(1, slots),
        owner_element_index,
        proj_blocks,
        second,
        group,
        capacity,
        direct,
    )
    first, received = section(states, 1, second, received, 0.25, [], True)
    (result,) = section(
        states, 0, first, received, 1.0, [(begin, 1.0 / 3.0), (second, 0.75)], False
    )

    tiles = tuple((0, m) for m in range(4))
    x_out, (inner,) = project(
        result, [outer], placing, extra, tiles, outputs, load=(proj_blocks, (16, 32))
    )
    rest_out, (adj_new,) = project(
        result, [inner], placing, extra, tiles, outputs, with_copy=True
    )
    send = send_chips if direct else lambda out: send_all(out, group, capacity)
    x_in = send(x_out)
    rest_in = send(rest_out)
    firsts = group // 2 if direct else 0
    cross = send_cores if direct else lambda blocks: blocks

    def rows_of(tiles):
        return jax.ShapeDtypeStruct((len(tiles) * VARS * 8, columns), jnp.float32)

    faces = face_shapes(columns)
    x_in = cross(x_in)
    x_part, *x_faces = receive(
        receive_x_kernel, x_in, [rows_of(X_TILES)] + faces[:2], len(x_in), firsts
    )
    xb, xa = exchange_x(x_faces)
    rest_in = cross(rest_in)
    adj_proj, *y_faces = receive(
        receive_rest_kernel,
        rest_in + [x_part],
        [jax.ShapeDtypeStruct((VARS, 64, columns), jnp.float32)] + faces[2:],
        len(rest_in),
        firsts,
        columns // LANES,
    )
    yb, ya = exchange_y(y_faces)
    adj_old = reverse_step(old_states[0], adj_proj, (xa, xb, ya, yb))
    return (adj_new.reshape(adj_final.shape), adj_old.reshape(adj_final.shape))


def solution(mesh):
    in_specs = (
        P("gx", None, None, ("gy", "gz")),
        P("gx", None, None, None, ("gy", "gz")),
        P("gx", None, None, None, ("gy", "gz")),
        P("gx", ("gy", "gz"), None),
        P("gx", ("gy", "gz")),
        P("gx", None, None, ("gy", "gz")),
    )
    out_specs = (P("gx", None, None, ("gy", "gz")), P("gx", None, None, ("gy", "gz")))
    return jax.shard_map(
        per_device, mesh=mesh, in_specs=in_specs, out_specs=out_specs, check_vma=False
    )
```

```python
import functools

import jax
import jax.numpy as jnp
import numpy as np
from jax import lax
from jax.experimental import pallas as pl
from jax.experimental.pallas import tpu as pltpu
from jax.sharding import PartitionSpec as P

ELEMENTS_Z = 64

step_rate = 0.01
lift_scale = 6.0
half_lift = 3.0
vmem_limit = 24 * 1024 * 1024
VARS = 5
LANES = 128


def swapped(value, axis, offset):
    count = lax.axis_size(axis)
    pairs = []
    for source in range(count):
        up = source % 2 == offset
        pairs.append((source, (source + (1 if up else -1)) % count))
    return lax.ppermute(value, axis, pairs)


def even_places():
    along_x = lax.axis_index("gx")
    along_y = lax.axis_index("gy") * lax.axis_size("gz") + lax.axis_index("gz")
    return lax.rem(along_x, 2) == 0, lax.rem(along_y, 2) == 0


def lgl_matrix():
    points = np.array([-1.0, -1.0 / np.sqrt(5.0), 1.0 / np.sqrt(5.0), 1.0])
    factors = np.array(
        [np.prod([points[i] - points[j] for j in range(4) if j != i]) for i in range(4)]
    )
    deriv_table = np.zeros((4, 4))
    for i in range(4):
        for j in range(4):
            if i != j:
                deriv_table[i, j] = factors[i] / (factors[j] * (points[i] - points[j]))
    for i in range(4):
        deriv_table[i, i] = -np.sum(deriv_table[i])
    return deriv_table


face_table = lgl_matrix()
face_table[0, 0] += half_lift
face_table[3, 3] -= half_lift
assert np.max(np.abs(np.diag(face_table))) < 1e-12


def iotas():
    row = lax.broadcasted_iota(jnp.int32, (8, LANES), 0)
    lane = lax.broadcasted_iota(jnp.int32, (8, LANES), 1)
    return row, lane


def by_sublane(row, values):
    out = jnp.full((8, LANES), np.float32(values[7]))
    for s in range(6, -1, -1):
        out = jnp.where(row == s, np.float32(values[s]), out)
    return out


def tile_of(ref, v, i, j):
    lead = v if isinstance(v, tuple) else (v,)
    return ref[lead + (slice(8 * i, 8 * i + 8), slice(LANES * j, LANES * (j + 1)))]


def primitive_state(get):
    inverse = 1.0 / get(0)
    speeds = [get(1 + d) * inverse for d in range(3)]
    kinetic = (
        get(1) * speeds[0] + get(2) * speeds[1] + get(3) * speeds[2]
    )
    energy = get(4)
    pressure = 0.4 * (energy - 0.5 * kinetic)
    return speeds, (energy + pressure) * inverse


def pull_full(speeds, enthalpy, v):
    total = v[0][4] * speeds[0] + v[1][4] * speeds[1] + v[2][4] * speeds[2]
    weight = v[0][1] + v[1][2] + v[2][3] + total
    fifth = 0.2 * weight
    pulled = []
    for d in range(3):
        part = (
            v[d][1] * speeds[0]
            + v[d][2] * speeds[1]
            + v[d][3] * speeds[2]
            + v[d][4] * enthalpy
        )
        pulled.append(part - fifth * speeds[d])
    out = [-(pulled[0] * speeds[0] + pulled[1] * speeds[1] + pulled[2] * speeds[2])]
    for j in range(3):
        moved = (
            v[0][1 + j] * speeds[0] + v[1][1 + j] * speeds[1] + v[2][1 + j] * speeds[2]
        )
        out.append(v[j][0] + moved - fifth * speeds[j] + pulled[j])
    out.append(total + 2.0 * fifth)
    return out


def pull_one(direction, speeds, enthalpy, v):
    own = speeds[direction]
    total = v[4] * own
    fifth = 0.2 * (v[1 + direction] + total)
    pulled = [-fifth * speeds[d] for d in range(3)]
    pulled[direction] = (
        v[1] * speeds[0]
        + v[2] * speeds[1]
        + v[3] * speeds[2]
        + v[4] * enthalpy
        + pulled[direction]
    )
    out = [-(pulled[0] * speeds[0] + pulled[1] * speeds[1] + pulled[2] * speeds[2])]
    for j in range(3):
        moved = v[1 + j] * own - fifth * speeds[j] + pulled[j]
        out.append(v[0] + moved if j == direction else moved)
    out.append(total + 2.0 * fifth)
    return out


def local_kernel(scale, index, extras, halves, spans, *refs):
    state_ref, w_ref = refs[0], refs[1]
    extra_refs = refs[2 : 2 + len(extras)]
    copies = []
    if spans:
        block_ref, out_ref, loaded_ref, sems = refs[2 + len(extras) :]
        at = 0
        for number, (start, size) in enumerate(spans):
            copies.append(
                pltpu.make_async_copy(
                    block_ref.at[0, :, start : start + size, :],
                    loaded_ref.at[:, at : at + size, :],
                    sems.at[number],
                )
            )
            copies[-1].start()
            at += size
    else:
        out_ref = refs[2 + len(extras)]
    row, lane = iotas()
    low_half_rows = row < 4
    low_half_lanes = lane < 64
    z_first = lane % ELEMENTS_Z == 0
    z_last = lane % ELEMENTS_Z == ELEMENTS_Z - 1
    z_shift = {}
    for k in (1, 2, 3, -1, -2, -3):
        column = [
            face_table[s % 4 - k, s % 4] if 0 <= s % 4 - k <= 3 else 0.0 for s in range(8)
        ]
        z_shift[k] = by_sublane(row, column)
    z_low = by_sublane(row, [half_lift if s % 4 == 0 else 0.0 for s in range(8)])
    z_high = by_sublane(row, [-half_lift if s % 4 == 3 else 0.0 for s in range(8)])
    zero = jnp.zeros((8, LANES), jnp.float32)

    for j in range(halves):
        for i in range(8):
            a, t = i // 2, i % 2
            other = 2 * a + 1 - t
            bs = [2 * t + s // 4 for s in range(8)]
            y_same = by_sublane(row, [face_table[2 * (1 - t) + s // 4, bs[s]] for s in range(8)])
            y_swap = by_sublane(row, [face_table[2 * t + 1 - s // 4, bs[s]] for s in range(8)])
            y_both = by_sublane(
                row, [face_table[2 * (1 - t) + 1 - s // 4, bs[s]] for s in range(8)]
            )
            y_face_rows = low_half_rows if t == 0 else jnp.logical_not(low_half_rows)
            y_sign = half_lift if t == 0 else -half_lift
            y_face = jnp.where(y_face_rows, np.float32(y_sign), 0.0)
            count = by_sublane(
                row,
                [
                    lift_scale
                    * ((a in (0, 3)) + (bs[s] in (0, 3)) + (s % 4 in (0, 3)))
                    for s in range(8)
                ],
            )
            v = [[], [], []]
            penalties = []
            for var in range(VARS):
                w = tile_of(w_ref, var, i, j)
                acc = None
                for source in range(4):
                    if source == a:
                        continue
                    term = np.float32(face_table[source, a]) * tile_of(
                        w_ref, var, 2 * source + t, j
                    )
                    acc = term if acc is None else acc + term
                v[0].append(acc)
                pair = tile_of(w_ref, var, other, j)
                pair_swapped = pltpu.roll(pair, 4, 0)
                acc = (
                    y_same * pair
                    + y_swap * pltpu.roll(w, 4, 0)
                    + y_both * pair_swapped
                )
                here = pltpu.roll(pair_swapped, 64, 1)
                if t == 0:
                    before = (
                        pltpu.roll(pltpu.roll(tile_of(w_ref, var, other, j - 1), 4, 0), 64, 1)
                        if j > 0
                        else zero
                    )
                    y_in = jnp.where(low_half_lanes, before, here)
                else:
                    after = (
                        pltpu.roll(pltpu.roll(tile_of(w_ref, var, other, j + 1), 4, 0), 64, 1)
                        if j < halves - 1
                        else zero
                    )
                    y_in = jnp.where(low_half_lanes, here, after)
                y_term = y_face * y_in
                v[1].append(acc + y_term)
                acc = None
                moved = {}
                for k in (1, 2, 3, -1, -2, -3):
                    moved[k] = pltpu.roll(w, k % 8, 0)
                    term = z_shift[k] * moved[k]
                    acc = term if acc is None else acc + term
                below = jnp.where(
                    z_first, pltpu.roll(moved[-3], 65, 1), pltpu.roll(moved[-3], 1, 1)
                )
                above = jnp.where(
                    z_last, pltpu.roll(moved[3], 63, 1), pltpu.roll(moved[3], 127, 1)
                )
                low_term = z_low * below
                high_term = z_high * above
                v[2].append(acc + low_term + high_term)
                y_jump = y_term if t == 0 else -y_term
                penalties.append(
                    count * w - 2.0 * (y_jump + (low_term - high_term))
                )
            speeds, enthalpy = primitive_state(lambda q: tile_of(state_ref, (index, q), i, j))
            pulled = pull_full(speeds, enthalpy, v)
            for var in range(VARS):
                change = (-step_rate * scale) * (pulled[var] + penalties[var])
                base = scale * tile_of(w_ref, var, i, j)
                for ref, factor in zip(extra_refs, extras):
                    base = base + np.float32(factor) * tile_of(ref, var, i, j)
                out_ref[var, 8 * i : 8 * i + 8, LANES * j : LANES * (j + 1)] = base + change
    for copy in copies:
        copy.wait()


def pack_x(lower, upper, xa_ref, xb_ref):
    even_x, _ = even_places()
    for var in range(VARS):
        xa_ref[var] = jnp.where(even_x, upper[var], lower[var])
        xb_ref[var] = jnp.where(even_x, lower[var], upper[var])


def pack_y(low_of, high_of, ya_ref, yb_ref):
    _, even_y = even_places()
    row, lane = iotas()
    low_rows = row < 4
    low_lanes = lane < 64
    for var in range(VARS):
        low = [low_of(var, a) for a in range(4)]
        left = jnp.where(low_rows, low[0], pltpu.roll(low[1], 4, 0))
        right = jnp.where(low_rows, low[2], pltpu.roll(low[3], 4, 0))
        lower = jnp.where(low_lanes, left, pltpu.roll(right, 64, 1))
        high = [high_of(var, a) for a in range(4)]
        left = jnp.where(low_rows, pltpu.roll(high[0], 4, 0), high[1])
        right = jnp.where(low_rows, pltpu.roll(high[2], 4, 0), high[3])
        upper = jnp.where(low_lanes, pltpu.roll(left, 64, 1), right)
        ya_ref[var] = jnp.where(even_y, upper, lower)
        yb_ref[var] = jnp.where(even_y, lower, upper)


def pack_faces(w_ref, halves, xa_ref, xb_ref, ya_ref, yb_ref):
    lower = [w_ref[var, 0:16, :] for var in range(VARS)]
    upper = [w_ref[var, 48:64, :] for var in range(VARS)]
    pack_x(lower, upper, xa_ref, xb_ref)
    pack_y(
        lambda var, a: tile_of(w_ref, var, 2 * a, 0),
        lambda var, a: tile_of(w_ref, var, 2 * a + 1, halves - 1),
        ya_ref,
        yb_ref,
    )


def face_kernel(halves, w_hbm, state_hbm, w_ref, state_ref, *refs):
    sems = refs[-1]
    first = pltpu.make_async_copy(w_hbm.at[0], w_ref, sems.at[0])
    second = pltpu.make_async_copy(state_hbm.at[0], state_ref, sems.at[1])
    first.start()
    second.start()
    first.wait()
    pack_faces(w_ref, halves, *refs[:-1])
    second.wait()


def finish_kernel(
    scale, index, skip, halves, state_ref, base_ref, xa_ref, xb_ref, ya_ref, yb_ref, *outs
):
    outs = outs[skip:]
    out_ref = outs[0]
    even_x, even_y = even_places()
    row, lane = iotas()
    rate = np.float32(-step_rate * scale)
    y_low_mask = jnp.where(jnp.logical_and(row < 4, lane < 64), np.float32(half_lift), 0.0)
    y_high_mask = jnp.where(jnp.logical_and(row >= 4, lane >= 64), np.float32(-half_lift), 0.0)
    for j in range(halves):
        for i in range(8):
            a, t = i // 2, i % 2
            has_x = a in (0, 3)
            has_y = (t == 0 and j == 0) or (t == 1 and j == halves - 1)
            place = (slice(8 * i, 8 * i + 8), slice(LANES * j, LANES * (j + 1)))
            values = [base_ref[(var,) + place] for var in range(VARS)]
            if has_x or has_y:
                speeds, enthalpy = primitive_state(lambda q: tile_of(state_ref, (index, q), i, j))
            if has_x:
                first = jnp.logical_not(even_x) if a == 0 else even_x
                sign = half_lift if a == 0 else -half_lift
                got = [
                    np.float32(sign)
                    * jnp.where(first, tile_of(xa_ref, var, t, j), tile_of(xb_ref, var, t, j))
                    for var in range(VARS)
                ]
                pulled = pull_one(0, speeds, enthalpy, got)
                jump = 2.0 if a == 0 else -2.0
                values = [
                    x + rate * (g - jump * q) for x, g, q in zip(values, pulled, got)
                ]
            if has_y:
                got = []
                for var in range(VARS):
                    first = jnp.logical_not(even_y) if t == 0 else even_y
                    packed = jnp.where(first, ya_ref[var], yb_ref[var])
                    if t == 0:
                        if a >= 2:
                            packed = pltpu.roll(packed, 64, 1)
                        if a % 2 == 1:
                            packed = pltpu.roll(packed, 4, 0)
                        got.append(y_low_mask * packed)
                    else:
                        if a < 2:
                            packed = pltpu.roll(packed, 64, 1)
                        if a % 2 == 0:
                            packed = pltpu.roll(packed, 4, 0)
                        got.append(y_high_mask * packed)
                pulled = pull_one(1, speeds, enthalpy, got)
                jump = 2.0 if t == 0 else -2.0
                values = [
                    x + rate * (g - jump * q) for x, g, q in zip(values, pulled, got)
                ]
            for var in range(VARS):
                out_ref[(var,) + place] = values[var]
    if len(outs) > 1:
        pack_faces(out_ref, halves, *outs[1:])


def vmem_spec():
    return pl.BlockSpec(memory_space=pltpu.VMEM)


def params():
    return pltpu.CompilerParams(vmem_limit_bytes=vmem_limit)


def face_shapes(columns):
    return [
        jax.ShapeDtypeStruct((VARS, 16, columns), jnp.float32),
        jax.ShapeDtypeStruct((VARS, 16, columns), jnp.float32),
        jax.ShapeDtypeStruct((VARS, 8, LANES), jnp.float32),
        jax.ShapeDtypeStruct((VARS, 8, LANES), jnp.float32),
    ]


def in_hbm(x):
    return pltpu.with_memory_space_constraint(x, pltpu.HBM)


def hbm_spec():
    return pl.BlockSpec(memory_space=pltpu.HBM)


def get_faces(w, states):
    columns = w.shape[3]
    shapes = [
        jax.ShapeDtypeStruct(w.shape[1:], jnp.float32),
        jax.ShapeDtypeStruct(states.shape[1:], jnp.float32),
    ] + face_shapes(columns)
    begin, states, *faces = pl.pallas_call(
        functools.partial(face_kernel, columns // LANES),
        out_shape=shapes,
        in_specs=[hbm_spec()] * 2,
        out_specs=[vmem_spec()] * len(shapes),
        scratch_shapes=[pltpu.SemaphoreType.DMA((2,))],
        compiler_params=params(),
        name="faces",
    )(in_hbm(w), in_hbm(states))
    return begin, states, faces


def prepare_kernel(group, direct, owner_ref, local_ref, after_ref, placing_ref, extra_ref):
    del after_ref
    places, slots = placing_ref.shape
    capacity = places // group
    target = owner_ref[...]
    if direct:
        here = lax.axis_index("gy") * lax.axis_size("gz") + lax.axis_index("gz")
        target = jnp.bitwise_xor(target, here)
    owner = lax.broadcasted_iota(jnp.int32, (group, slots), 0)
    named = jnp.where(owner == target, np.float32(1), np.float32(0))
    earlier = jnp.where(
        lax.broadcasted_iota(jnp.int32, (slots, slots), 0)
        < lax.broadcasted_iota(jnp.int32, (slots, slots), 1),
        np.float32(1),
        np.float32(0),
    )
    ranks = jnp.dot(
        named.astype(jnp.bfloat16),
        earlier.astype(jnp.bfloat16),
        preferred_element_type=jnp.float32,
    )
    rank = jnp.sum(named * ranks, axis=0, keepdims=True).astype(jnp.int32)
    place = target * capacity + rank
    index = lax.broadcasted_iota(jnp.int32, (places, slots), 0)
    placing_ref[...] = jnp.where(index == place, np.float32(1), np.float32(0)).astype(
        jnp.bfloat16
    )
    extra_ref[...] = jnp.broadcast_to(local_ref[...].astype(jnp.float32), extra_ref.shape)


def prepare(owners, local, after, group, capacity, direct):
    slots = local.shape[1]
    return pl.pallas_call(
        functools.partial(prepare_kernel, group, direct),
        out_shape=[
            jax.ShapeDtypeStruct((group * capacity, slots), jnp.bfloat16),
            jax.ShapeDtypeStruct((8, slots), jnp.float32),
        ],
        in_specs=[vmem_spec()] * 3,
        out_specs=[vmem_spec()] * 2,
        compiler_params=params(),
        name="prepare",
    )(owners, local, after)


def exchange_x(faces):
    return swapped(faces[1], "gx", 1), swapped(faces[0], "gx", 0)


def exchange_y(faces):
    ring = ("gy", "gz")
    return swapped(faces[1], ring, 1), swapped(faces[0], ring, 0)


def exchange(faces):
    xb, xa = exchange_x(faces[:2])
    yb, ya = exchange_y(faces[2:])
    return xa, xb, ya, yb


def section(states, index, w, received, scale, extras, with_faces, load=None, after=()):
    columns = w.shape[2]
    halves = columns // LANES
    shape = jax.ShapeDtypeStruct(w.shape, jnp.float32)
    factors = tuple(f for _, f in extras)
    operands = [states, w] + [x for x, _ in extras]
    in_specs = [vmem_spec()] * len(operands)
    out_shape = [shape]
    scratch = []
    spans = ()
    if load is not None:
        blocks, spans = load
        operands.append(in_hbm(blocks))
        in_specs.append(hbm_spec())
        nodes = sum(size for _, size in spans)
        out_shape.append(jax.ShapeDtypeStruct((64, nodes, blocks.shape[3]), jnp.float32))
        scratch = [pltpu.SemaphoreType.DMA((len(spans),))]
    base, *loaded = pl.pallas_call(
        functools.partial(local_kernel, scale, index, factors, halves, spans),
        out_shape=out_shape,
        in_specs=in_specs,
        out_specs=[vmem_spec()] * len(out_shape),
        scratch_shapes=scratch,
        compiler_params=params(),
        cost_estimate=pl.CostEstimate(
            flops=400 * 64 * columns, bytes_accessed=12 * VARS * 64 * columns, transcendentals=0
        ),
        name="local_part",
    )(*operands)
    out_shape = [shape] + (face_shapes(columns) if with_faces else [])
    results = pl.pallas_call(
        functools.partial(finish_kernel, scale, index, len(after), halves),
        out_shape=out_shape,
        in_specs=[vmem_spec()] * (6 + len(after)),
        out_specs=[vmem_spec()] * len(out_shape),
        compiler_params=params(),
        name="finish",
    )(states, base, *received, *after)
    if with_faces:
        results = [results[0], exchange(results[1:])]
    return list(results) + loaded


def reverse_step(states, begin, received):
    second, received = section(states, 2, begin, received, 2.0 / 3.0, [], True)
    first, received = section(states, 1, second, received, 0.25, [], True)
    (result,) = section(
        states, 0, first, received, 1.0, [(begin, 1.0 / 3.0), (second, 0.75)], False
    )
    return result


def split_two(x):
    high = x.astype(jnp.bfloat16)
    low = (x - high.astype(jnp.float32)).astype(jnp.bfloat16)
    return high, low


X_TILES = (0, 1, 6, 7)
REST_TILES = (2, 3, 4, 5)


def project_kernel(tiles, sources, blocks, span, with_copy, *refs):
    w_ref = refs[0]
    block_refs = refs[1 : 1 + sources]
    placing_ref, extra_ref = refs[1 + sources : 3 + sources]
    at = 3 + sources + (1 if span else 0)
    out_refs = refs[at : at + blocks]
    held, sem = refs[-2:]
    if with_copy:
        copy = pltpu.make_async_copy(w_ref, refs[at + blocks], sem.at[0])
        copy.start()
    if span:
        start, size = span
        copy = pltpu.make_async_copy(
            refs[at - 1].at[0, :, start : start + size, :], refs[at + blocks], sem.at[0]
        )
        copy.start()
    halves = w_ref.shape[2] // LANES
    count = len(tiles) * VARS
    for r in range(placing_ref.shape[1] // LANES):
        lanes = slice(LANES * r, LANES * (r + 1))
        half = r % halves
        w_lanes = slice(LANES * half, LANES * (half + 1))

        def body(tile, sums):
            start = pl.multiple_of(8 * tile, 8)
            groups = [w_ref[var, pl.ds(start, 8), w_lanes] for var in range(VARS)]
            sums = list(sums)
            for s in range(8):
                rows = [jnp.broadcast_to(group[s : s + 1], (8, LANES)) for group in groups]
                for m, (source, at) in enumerate(tiles):
                    block = block_refs[source][start + s, 8 * at : 8 * at + 8, lanes]
                    for var in range(VARS):
                        q = m * VARS + var
                        sums[q] = sums[q] + block * rows[var]
            return tuple(sums)

        start = tuple(jnp.zeros((8, LANES), jnp.float32) for _ in range(count))
        sums = lax.fori_loop(0, 8, body, start)
        for q in range(count):
            held[8 * q : 8 * q + 8, lanes] = sums[q]

    values = jnp.concatenate([held[...], extra_ref[...]], axis=0)
    total = values.shape[0]
    pieces = jnp.concatenate(split_two(values), axis=0)
    result = lax.dot_general(
        pieces,
        placing_ref[...],
        (((1,), (1,)), ((), ())),
        preferred_element_type=jnp.float32,
    )
    result = result[0:total] + result[total:]
    per = result.shape[1] // blocks
    for g in range(blocks):
        for part in range(per // LANES):
            at = per * g + LANES * part
            out_refs[g][part] = result[:, at : at + LANES]
    if with_copy or span:
        copy.wait()


def project(w, sources, placing, extra, tiles, outputs, load=None, with_copy=False):
    slots = placing.shape[1]
    rows = len(tiles) * VARS * 8
    per = placing.shape[0] // outputs // LANES
    operands = [w, *sources, placing, extra]
    in_specs = [vmem_spec()] * len(operands)
    out_shape = [jax.ShapeDtypeStruct((per, rows + 8, LANES), jnp.float32)] * outputs
    out_specs = [vmem_spec()] * outputs
    span = None
    if load is not None:
        blocks, span = load
        operands.append(in_hbm(blocks))
        in_specs.append(hbm_spec())
        out_shape.append(jax.ShapeDtypeStruct((64, span[1], slots), jnp.float32))
        out_specs.append(vmem_spec())
    if with_copy:
        out_shape.append(jax.ShapeDtypeStruct(w.shape, jnp.float32))
        out_specs.append(pl.BlockSpec(memory_space=pl.ANY))
    results = pl.pallas_call(
        functools.partial(project_kernel, tiles, len(sources), outputs, span, with_copy),
        out_shape=out_shape,
        in_specs=in_specs,
        out_specs=out_specs,
        scratch_shapes=[
            pltpu.VMEM((rows, slots), jnp.float32),
            pltpu.SemaphoreType.DMA((1,)),
        ],
        compiler_params=params(),
        cost_estimate=pl.CostEstimate(
            flops=1000 * 1000 * 1000 * len(tiles),
            bytes_accessed=4 * rows * 64 * slots,
            transcendentals=0,
        ),
        name="project",
    )(*operands)
    return results[:outputs], results[outputs:]


def add_slots(block_refs, firsts, rows, columns):
    result = jnp.zeros((rows, columns), jnp.float32)
    index = lax.broadcasted_iota(jnp.int32, (columns, LANES), 0)
    for number, ref in enumerate(block_refs):
        for g in range(1 if number < firsts else ref.shape[0]):
            local = ref[g, rows : rows + 1, :].astype(jnp.int32)
            spot = (index == local).astype(jnp.float32).astype(jnp.bfloat16)
            for piece in split_two(ref[g, 0:rows, :]):
                result = result + lax.dot_general(
                    piece, spot, (((1,), (1,)), ((), ())), preferred_element_type=jnp.float32
                )
    return result


def receive_x_kernel(count, firsts, *refs):
    out_ref, xa_ref, xb_ref = refs[count:]
    rows, columns = out_ref.shape
    result = add_slots(refs[:count], firsts, rows, columns)
    out_ref[...] = result

    def tile(m, var):
        q = m * VARS + var
        return result[8 * q : 8 * q + 8]

    lower = [jnp.concatenate([tile(0, v), tile(1, v)], axis=0) for v in range(VARS)]
    upper = [jnp.concatenate([tile(2, v), tile(3, v)], axis=0) for v in range(VARS)]
    pack_x(lower, upper, xa_ref, xb_ref)


def receive_rest_kernel(count, firsts, halves, *refs):
    x_ref, out_ref, ya_ref, yb_ref = refs[count:]
    columns = out_ref.shape[2]
    rest = add_slots(refs[:count], firsts, len(REST_TILES) * VARS * 8, columns)
    for var in range(VARS):
        for m, tile in enumerate(X_TILES):
            q = 8 * (m * VARS + var)
            out_ref[var, 8 * tile : 8 * tile + 8, :] = x_ref[q : q + 8, :]
        for m, tile in enumerate(REST_TILES):
            q = 8 * (m * VARS + var)
            out_ref[var, 8 * tile : 8 * tile + 8, :] = rest[q : q + 8]
    pack_y(
        lambda var, a: tile_of(out_ref, var, 2 * a, 0),
        lambda var, a: tile_of(out_ref, var, 2 * a + 1, halves - 1),
        ya_ref,
        yb_ref,
    )


def receive(kernel, operands, shapes, *settings):
    return pl.pallas_call(
        functools.partial(kernel, *settings),
        out_shape=shapes,
        in_specs=[vmem_spec()] * len(operands),
        out_specs=[vmem_spec()] * len(shapes),
        compiler_params=params(),
        cost_estimate=pl.CostEstimate(
            flops=1000 * 1000 * 1000, bytes_accessed=1000 * 1000, transcendentals=0
        ),
        name="receive",
    )(*operands)


def send_chips(values):
    ring = ("gy", "gz")
    count = len(values)
    mine = [values[0]] * count
    for d in range(count - 1, 0, -1):
        pairs = [(s, s ^ (2 * d)) for s in range(2 * count)]
        mine[d] = lax.ppermute(values[d], ring, pairs)
    return mine


def send_cores(mine):
    others = jnp.concatenate([part[1:2] for part in mine], axis=0)
    pairs = [(s, s ^ 1) for s in range(2 * len(mine))]
    return mine + [lax.ppermute(others, ("gy", "gz"), pairs)]


def send_all(values, group, capacity):
    (values,) = values
    blocks, rows, lanes = values.shape
    per = lanes // capacity
    values = values.reshape(blocks, rows, per, capacity).transpose(0, 2, 1, 3)
    values = values.reshape(group, rows, capacity)
    values = lax.all_to_all(values, ("gy", "gz"), split_axis=0, concat_axis=0, tiled=True)
    values = values.reshape(blocks, per, rows, capacity).transpose(0, 2, 1, 3)
    return [values.reshape(blocks, rows, lanes)]


def per_device(
    adj_final, new_states, old_states, owner_device_index, owner_element_index, proj_blocks
):
    columns = adj_final.shape[3]
    slots = proj_blocks.shape[3]
    group = lax.axis_size("gy") * lax.axis_size("gz")
    capacity = max(2, (2 * slots + group - 1) // group)
    begin, states, faces = get_faces(adj_final, new_states)
    received = exchange(faces)
    second, received = section(states, 2, begin, received, 2.0 / 3.0, [], True)

    direct = group in (2, 4, 8) and capacity == LANES
    outputs = group // 2 if direct else 1
    placing, extra = prepare(
        owner_device_index.reshape(1, slots),
        owner_element_index,
        second,
        group,
        capacity,
        direct,
    )
    first, received = section(
        states, 1, second, received, 0.25, [], True, after=[extra]
    )
    result, outer = section(
        states,
        0,
        first,
        received,
        1.0,
        [(begin, 1.0 / 3.0), (second, 0.75)],
        False,
        load=(proj_blocks, ((0, 16), (48, 16))),
    )

    tiles = tuple((0, m) for m in range(4))
    x_out, (inner,) = project(
        result, [outer], placing, extra, tiles, outputs, load=(proj_blocks, (16, 32))
    )
    rest_out, (adj_new,) = project(
        result, [inner], placing, extra, tiles, outputs, with_copy=True
    )
    send = send_chips if direct else lambda out: send_all(out, group, capacity)
    x_in = send(x_out)
    rest_in = send(rest_out)
    firsts = group // 2 if direct else 0
    cross = send_cores if direct else lambda blocks: blocks

    def rows_of(tiles):
        return jax.ShapeDtypeStruct((len(tiles) * VARS * 8, columns), jnp.float32)

    faces = face_shapes(columns)
    x_in = cross(x_in)
    x_part, *x_faces = receive(
        receive_x_kernel, x_in, [rows_of(X_TILES)] + faces[:2], len(x_in), firsts
    )
    xb, xa = exchange_x(x_faces)
    rest_in = cross(rest_in)
    adj_proj, *y_faces = receive(
        receive_rest_kernel,
        rest_in + [x_part],
        [jax.ShapeDtypeStruct((VARS, 64, columns), jnp.float32)] + faces[2:],
        len(rest_in),
        firsts,
        columns // LANES,
    )
    yb, ya = exchange_y(y_faces)
    adj_old = reverse_step(old_states[0], adj_proj, (xa, xb, ya, yb))
    return (adj_new.reshape(adj_final.shape), adj_old.reshape(adj_final.shape))


def solution(mesh):
    in_specs = (
        P("gx", None, None, ("gy", "gz")),
        P("gx", None, None, None, ("gy", "gz")),
        P("gx", None, None, None, ("gy", "gz")),
        P("gx", ("gy", "gz"), None),
        P("gx", ("gy", "gz")),
        P("gx", None, None, ("gy", "gz")),
    )
    out_specs = (P("gx", None, None, ("gy", "gz")), P("gx", None, None, ("gy", "gz")))
    return jax.shard_map(
        per_device, mesh=mesh, in_specs=in_specs, out_specs=out_specs, check_vma=False
    )
```

```python
import functools

import jax
import jax.numpy as jnp
import numpy as np
from jax import lax
from jax.experimental import pallas as pl
from jax.experimental.pallas import tpu as pltpu
from jax.sharding import PartitionSpec as P

ELEMENTS_Z = 64

step_rate = 0.01
lift_scale = 6.0
half_lift = 3.0
vmem_limit = 24 * 1024 * 1024
VARS = 5
LANES = 128


def swapped(value, axis, offset):
    count = lax.axis_size(axis)
    pairs = []
    for source in range(count):
        up = source % 2 == offset
        pairs.append((source, (source + (1 if up else -1)) % count))
    return lax.ppermute(value, axis, pairs)


def even_places():
    along_x = lax.axis_index("gx")
    along_y = lax.axis_index("gy") * lax.axis_size("gz") + lax.axis_index("gz")
    return lax.rem(along_x, 2) == 0, lax.rem(along_y, 2) == 0


def lgl_matrix():
    points = np.array([-1.0, -1.0 / np.sqrt(5.0), 1.0 / np.sqrt(5.0), 1.0])
    factors = np.array(
        [np.prod([points[i] - points[j] for j in range(4) if j != i]) for i in range(4)]
    )
    deriv_table = np.zeros((4, 4))
    for i in range(4):
        for j in range(4):
            if i != j:
                deriv_table[i, j] = factors[i] / (factors[j] * (points[i] - points[j]))
    for i in range(4):
        deriv_table[i, i] = -np.sum(deriv_table[i])
    return deriv_table


face_table = lgl_matrix()
face_table[0, 0] += half_lift
face_table[3, 3] -= half_lift
assert np.max(np.abs(np.diag(face_table))) < 1e-12


def iotas():
    row = lax.broadcasted_iota(jnp.int32, (8, LANES), 0)
    lane = lax.broadcasted_iota(jnp.int32, (8, LANES), 1)
    return row, lane


def by_sublane(row, values):
    out = jnp.full((8, LANES), np.float32(values[7]))
    for s in range(6, -1, -1):
        out = jnp.where(row == s, np.float32(values[s]), out)
    return out


def tile_of(ref, v, i, j):
    lead = v if isinstance(v, tuple) else (v,)
    return ref[lead + (slice(8 * i, 8 * i + 8), slice(LANES * j, LANES * (j + 1)))]


def primitive_state(get):
    inverse = 1.0 / get(0)
    speeds = [get(1 + d) * inverse for d in range(3)]
    kinetic = (
        get(1) * speeds[0] + get(2) * speeds[1] + get(3) * speeds[2]
    )
    energy = get(4)
    pressure = 0.4 * (energy - 0.5 * kinetic)
    return speeds, (energy + pressure) * inverse


def pull_full(speeds, enthalpy, v):
    total = v[0][4] * speeds[0] + v[1][4] * speeds[1] + v[2][4] * speeds[2]
    weight = v[0][1] + v[1][2] + v[2][3] + total
    fifth = 0.2 * weight
    pulled = []
    for d in range(3):
        part = (
            v[d][1] * speeds[0]
            + v[d][2] * speeds[1]
            + v[d][3] * speeds[2]
            + v[d][4] * enthalpy
        )
        pulled.append(part - fifth * speeds[d])
    out = [-(pulled[0] * speeds[0] + pulled[1] * speeds[1] + pulled[2] * speeds[2])]
    for j in range(3):
        moved = (
            v[0][1 + j] * speeds[0] + v[1][1 + j] * speeds[1] + v[2][1 + j] * speeds[2]
        )
        out.append(v[j][0] + moved - fifth * speeds[j] + pulled[j])
    out.append(total + 2.0 * fifth)
    return out


def pull_one(direction, speeds, enthalpy, v):
    own = speeds[direction]
    total = v[4] * own
    fifth = 0.2 * (v[1 + direction] + total)
    pulled = [-fifth * speeds[d] for d in range(3)]
    pulled[direction] = (
        v[1] * speeds[0]
        + v[2] * speeds[1]
        + v[3] * speeds[2]
        + v[4] * enthalpy
        + pulled[direction]
    )
    out = [-(pulled[0] * speeds[0] + pulled[1] * speeds[1] + pulled[2] * speeds[2])]
    for j in range(3):
        moved = v[1 + j] * own - fifth * speeds[j] + pulled[j]
        out.append(v[0] + moved if j == direction else moved)
    out.append(total + 2.0 * fifth)
    return out


def local_kernel(scale, index, extras, halves, spans, *refs):
    state_ref, w_ref = refs[0], refs[1]
    extra_refs = refs[2 : 2 + len(extras)]
    copies = []
    if spans:
        block_ref, out_ref, loaded_ref, sems = refs[2 + len(extras) :]
        at = 0
        for number, (start, size) in enumerate(spans):
            copies.append(
                pltpu.make_async_copy(
                    block_ref.at[0, :, start : start + size, :],
                    loaded_ref.at[:, at : at + size, :],
                    sems.at[number],
                )
            )
            copies[-1].start()
            at += size
    else:
        out_ref = refs[2 + len(extras)]
    row, lane = iotas()
    low_half_rows = row < 4
    low_half_lanes = lane < 64
    z_first = lane % ELEMENTS_Z == 0
    z_last = lane % ELEMENTS_Z == ELEMENTS_Z - 1
    z_shift = {}
    for k in (1, 2, 3, -1, -2, -3):
        column = [
            face_table[s % 4 - k, s % 4] if 0 <= s % 4 - k <= 3 else 0.0 for s in range(8)
        ]
        z_shift[k] = by_sublane(row, column)
    z_low = by_sublane(row, [half_lift if s % 4 == 0 else 0.0 for s in range(8)])
    z_high = by_sublane(row, [-half_lift if s % 4 == 3 else 0.0 for s in range(8)])
    zero = jnp.zeros((8, LANES), jnp.float32)

    for j in range(halves):
        for i in range(8):
            a, t = i // 2, i % 2
            other = 2 * a + 1 - t
            bs = [2 * t + s // 4 for s in range(8)]
            y_same = by_sublane(row, [face_table[2 * (1 - t) + s // 4, bs[s]] for s in range(8)])
            y_swap = by_sublane(row, [face_table[2 * t + 1 - s // 4, bs[s]] for s in range(8)])
            y_both = by_sublane(
                row, [face_table[2 * (1 - t) + 1 - s // 4, bs[s]] for s in range(8)]
            )
            y_face_rows = low_half_rows if t == 0 else jnp.logical_not(low_half_rows)
            y_sign = half_lift if t == 0 else -half_lift
            y_face = jnp.where(y_face_rows, np.float32(y_sign), 0.0)
            count = by_sublane(
                row,
                [
                    lift_scale
                    * ((a in (0, 3)) + (bs[s] in (0, 3)) + (s % 4 in (0, 3)))
                    for s in range(8)
                ],
            )
            v = [[], [], []]
            penalties = []
            for var in range(VARS):
                w = tile_of(w_ref, var, i, j)
                acc = None
                for source in range(4):
                    if source == a:
                        continue
                    term = np.float32(face_table[source, a]) * tile_of(
                        w_ref, var, 2 * source + t, j
                    )
                    acc = term if acc is None else acc + term
                v[0].append(acc)
                pair = tile_of(w_ref, var, other, j)
                pair_swapped = pltpu.roll(pair, 4, 0)
                acc = (
                    y_same * pair
                    + y_swap * pltpu.roll(w, 4, 0)
                    + y_both * pair_swapped
                )
                here = pltpu.roll(pair_swapped, 64, 1)
                if t == 0:
                    before = (
                        pltpu.roll(pltpu.roll(tile_of(w_ref, var, other, j - 1), 4, 0), 64, 1)
                        if j > 0
                        else zero
                    )
                    y_in = jnp.where(low_half_lanes, before, here)
                else:
                    after = (
                        pltpu.roll(pltpu.roll(tile_of(w_ref, var, other, j + 1), 4, 0), 64, 1)
                        if j < halves - 1
                        else zero
                    )
                    y_in = jnp.where(low_half_lanes, here, after)
                y_term = y_face * y_in
                v[1].append(acc + y_term)
                acc = None
                moved = {}
                for k in (1, 2, 3, -1, -2, -3):
                    moved[k] = pltpu.roll(w, k % 8, 0)
                    term = z_shift[k] * moved[k]
                    acc = term if acc is None else acc + term
                below = jnp.where(
                    z_first, pltpu.roll(moved[-3], 65, 1), pltpu.roll(moved[-3], 1, 1)
                )
                above = jnp.where(
                    z_last, pltpu.roll(moved[3], 63, 1), pltpu.roll(moved[3], 127, 1)
                )
                low_term = z_low * below
                high_term = z_high * above
                v[2].append(acc + low_term + high_term)
                y_jump = y_term if t == 0 else -y_term
                penalties.append(
                    count * w - 2.0 * (y_jump + (low_term - high_term))
                )
            speeds, enthalpy = primitive_state(lambda q: tile_of(state_ref, (index, q), i, j))
            pulled = pull_full(speeds, enthalpy, v)
            for var in range(VARS):
                change = (-step_rate * scale) * (pulled[var] + penalties[var])
                base = scale * tile_of(w_ref, var, i, j)
                for ref, factor in zip(extra_refs, extras):
                    base = base + np.float32(factor) * tile_of(ref, var, i, j)
                out_ref[var, 8 * i : 8 * i + 8, LANES * j : LANES * (j + 1)] = base + change
    for copy in copies:
        copy.wait()


def pack_x(lower, upper, xa_ref, xb_ref):
    even_x, _ = even_places()
    for var in range(VARS):
        xa_ref[var] = jnp.where(even_x, upper[var], lower[var])
        xb_ref[var] = jnp.where(even_x, lower[var], upper[var])


def pack_y(low_of, high_of, ya_ref, yb_ref):
    _, even_y = even_places()
    row, lane = iotas()
    low_rows = row < 4
    low_lanes = lane < 64
    for var in range(VARS):
        low = [low_of(var, a) for a in range(4)]
        left = jnp.where(low_rows, low[0], pltpu.roll(low[1], 4, 0))
        right = jnp.where(low_rows, low[2], pltpu.roll(low[3], 4, 0))
        lower = jnp.where(low_lanes, left, pltpu.roll(right, 64, 1))
        high = [high_of(var, a) for a in range(4)]
        left = jnp.where(low_rows, pltpu.roll(high[0], 4, 0), high[1])
        right = jnp.where(low_rows, pltpu.roll(high[2], 4, 0), high[3])
        upper = jnp.where(low_lanes, pltpu.roll(left, 64, 1), right)
        ya_ref[var] = jnp.where(even_y, upper, lower)
        yb_ref[var] = jnp.where(even_y, lower, upper)


def pack_faces(w_ref, halves, xa_ref, xb_ref, ya_ref, yb_ref):
    lower = [w_ref[var, 0:16, :] for var in range(VARS)]
    upper = [w_ref[var, 48:64, :] for var in range(VARS)]
    pack_x(lower, upper, xa_ref, xb_ref)
    pack_y(
        lambda var, a: tile_of(w_ref, var, 2 * a, 0),
        lambda var, a: tile_of(w_ref, var, 2 * a + 1, halves - 1),
        ya_ref,
        yb_ref,
    )


def face_kernel(halves, w_hbm, state_hbm, w_ref, state_ref, *refs):
    sems = refs[-1]
    first = pltpu.make_async_copy(w_hbm.at[0], w_ref, sems.at[0])
    second = pltpu.make_async_copy(state_hbm.at[0], state_ref, sems.at[1])
    first.start()
    second.start()
    first.wait()
    pack_faces(w_ref, halves, *refs[:-1])
    second.wait()


def finish_kernel(
    scale, index, skip, halves, state_ref, base_ref, xa_ref, xb_ref, yb_ref, ya_ref, *outs
):
    outs = outs[skip:]
    out_ref = outs[0]
    even_x, even_y = even_places()
    row, lane = iotas()
    rate = np.float32(-step_rate * scale)
    y_low_mask = jnp.where(jnp.logical_and(row < 4, lane < 64), np.float32(half_lift), 0.0)
    y_high_mask = jnp.where(jnp.logical_and(row >= 4, lane >= 64), np.float32(-half_lift), 0.0)
    for j in range(halves):
        for i in range(8):
            a, t = i // 2, i % 2
            has_x = a in (0, 3)
            has_y = (t == 0 and j == 0) or (t == 1 and j == halves - 1)
            place = (slice(8 * i, 8 * i + 8), slice(LANES * j, LANES * (j + 1)))
            values = [base_ref[(var,) + place] for var in range(VARS)]
            if has_x or has_y:
                speeds, enthalpy = primitive_state(lambda q: tile_of(state_ref, (index, q), i, j))
            if has_x:
                first = jnp.logical_not(even_x) if a == 0 else even_x
                sign = half_lift if a == 0 else -half_lift
                got = [
                    np.float32(sign)
                    * jnp.where(first, tile_of(xa_ref, var, t, j), tile_of(xb_ref, var, t, j))
                    for var in range(VARS)
                ]
                pulled = pull_one(0, speeds, enthalpy, got)
                jump = 2.0 if a == 0 else -2.0
                values = [
                    x + rate * (g - jump * q) for x, g, q in zip(values, pulled, got)
                ]
            if has_y:
                got = []
                for var in range(VARS):
                    first = jnp.logical_not(even_y) if t == 0 else even_y
                    packed = jnp.where(first, ya_ref[var], yb_ref[var])
                    if t == 0:
                        if a >= 2:
                            packed = pltpu.roll(packed, 64, 1)
                        if a % 2 == 1:
                            packed = pltpu.roll(packed, 4, 0)
                        got.append(y_low_mask * packed)
                    else:
                        if a < 2:
                            packed = pltpu.roll(packed, 64, 1)
                        if a % 2 == 0:
                            packed = pltpu.roll(packed, 4, 0)
                        got.append(y_high_mask * packed)
                pulled = pull_one(1, speeds, enthalpy, got)
                jump = 2.0 if t == 0 else -2.0
                values = [
                    x + rate * (g - jump * q) for x, g, q in zip(values, pulled, got)
                ]
            for var in range(VARS):
                out_ref[(var,) + place] = values[var]
    if len(outs) > 1:
        pack_faces(out_ref, halves, *outs[1:])


def vmem_spec():
    return pl.BlockSpec(memory_space=pltpu.VMEM)


def params():
    return pltpu.CompilerParams(vmem_limit_bytes=vmem_limit)


def face_shapes(columns):
    return [
        jax.ShapeDtypeStruct((VARS, 16, columns), jnp.float32),
        jax.ShapeDtypeStruct((VARS, 16, columns), jnp.float32),
        jax.ShapeDtypeStruct((VARS, 8, LANES), jnp.float32),
        jax.ShapeDtypeStruct((VARS, 8, LANES), jnp.float32),
    ]


def in_hbm(x):
    return pltpu.with_memory_space_constraint(x, pltpu.HBM)


def hbm_spec():
    return pl.BlockSpec(memory_space=pltpu.HBM)


def get_faces(w, states):
    columns = w.shape[3]
    shapes = [
        jax.ShapeDtypeStruct(w.shape[1:], jnp.float32),
        jax.ShapeDtypeStruct(states.shape[1:], jnp.float32),
    ] + face_shapes(columns)
    begin, states, *faces = pl.pallas_call(
        functools.partial(face_kernel, columns // LANES),
        out_shape=shapes,
        in_specs=[hbm_spec()] * 2,
        out_specs=[vmem_spec()] * len(shapes),
        scratch_shapes=[pltpu.SemaphoreType.DMA((2,))],
        compiler_params=params(),
        name="faces",
    )(in_hbm(w), in_hbm(states))
    return begin, states, faces


def prepare_kernel(group, direct, owner_ref, local_ref, after_ref, placing_ref, extra_ref):
    del after_ref
    places, slots = placing_ref.shape
    capacity = places // group
    target = owner_ref[...]
    if direct:
        here = lax.axis_index("gy") * lax.axis_size("gz") + lax.axis_index("gz")
        target = jnp.bitwise_xor(target, here)
    owner = lax.broadcasted_iota(jnp.int32, (group, slots), 0)
    named = jnp.where(owner == target, np.float32(1), np.float32(0))
    earlier = jnp.where(
        lax.broadcasted_iota(jnp.int32, (slots, slots), 0)
        < lax.broadcasted_iota(jnp.int32, (slots, slots), 1),
        np.float32(1),
        np.float32(0),
    )
    ranks = jnp.dot(
        named.astype(jnp.bfloat16),
        earlier.astype(jnp.bfloat16),
        preferred_element_type=jnp.float32,
    )
    rank = jnp.sum(named * ranks, axis=0, keepdims=True).astype(jnp.int32)
    place = target * capacity + rank
    index = lax.broadcasted_iota(jnp.int32, (places, slots), 0)
    placing_ref[...] = jnp.where(index == place, np.float32(1), np.float32(0)).astype(
        jnp.bfloat16
    )
    extra_ref[...] = jnp.broadcast_to(local_ref[...].astype(jnp.float32), extra_ref.shape)


def prepare(owners, local, after, group, capacity, direct):
    slots = local.shape[1]
    return pl.pallas_call(
        functools.partial(prepare_kernel, group, direct),
        out_shape=[
            jax.ShapeDtypeStruct((group * capacity, slots), jnp.bfloat16),
            jax.ShapeDtypeStruct((8, slots), jnp.float32),
        ],
        in_specs=[vmem_spec()] * 3,
        out_specs=[vmem_spec()] * 2,
        compiler_params=params(),
        name="prepare",
    )(owners, local, after)


def exchange_x(faces):
    return swapped(faces[1], "gx", 1), swapped(faces[0], "gx", 0)


def exchange_y(faces):
    ring = ("gy", "gz")
    return swapped(faces[1], ring, 1), swapped(faces[0], ring, 0)


def exchange(faces):
    xb, xa = exchange_x(faces[:2])
    yb, ya = exchange_y(faces[2:])
    return xa, xb, yb, ya


def section(states, index, w, received, scale, extras, with_faces, load=None, after=()):
    columns = w.shape[2]
    halves = columns // LANES
    shape = jax.ShapeDtypeStruct(w.shape, jnp.float32)
    factors = tuple(f for _, f in extras)
    operands = [states, w] + [x for x, _ in extras]
    in_specs = [vmem_spec()] * len(operands)
    out_shape = [shape]
    scratch = []
    spans = ()
    if load is not None:
        blocks, spans = load
        operands.append(in_hbm(blocks))
        in_specs.append(hbm_spec())
        nodes = sum(size for _, size in spans)
        out_shape.append(jax.ShapeDtypeStruct((64, nodes, blocks.shape[3]), jnp.float32))
        scratch = [pltpu.SemaphoreType.DMA((len(spans),))]
    base, *loaded = pl.pallas_call(
        functools.partial(local_kernel, scale, index, factors, halves, spans),
        out_shape=out_shape,
        in_specs=in_specs,
        out_specs=[vmem_spec()] * len(out_shape),
        scratch_shapes=scratch,
        compiler_params=params(),
        cost_estimate=pl.CostEstimate(
            flops=400 * 64 * columns, bytes_accessed=12 * VARS * 64 * columns, transcendentals=0
        ),
        name="local_part",
    )(*operands)
    out_shape = [shape] + (face_shapes(columns) if with_faces else [])
    results = pl.pallas_call(
        functools.partial(finish_kernel, scale, index, len(after), halves),
        out_shape=out_shape,
        in_specs=[vmem_spec()] * (6 + len(after)),
        out_specs=[vmem_spec()] * len(out_shape),
        compiler_params=params(),
        name="finish",
    )(states, base, *received, *after)
    if with_faces:
        results = [results[0], exchange(results[1:])]
    return list(results) + loaded


def reverse_step(states, begin, received):
    second, received = section(states, 2, begin, received, 2.0 / 3.0, [], True)
    first, received = section(states, 1, second, received, 0.25, [], True)
    (result,) = section(
        states, 0, first, received, 1.0, [(begin, 1.0 / 3.0), (second, 0.75)], False
    )
    return result


def split_two(x):
    high = x.astype(jnp.bfloat16)
    low = (x - high.astype(jnp.float32)).astype(jnp.bfloat16)
    return high, low


X_TILES = (0, 1, 6, 7)
REST_TILES = (2, 3, 4, 5)


def project_kernel(tiles, sources, blocks, span, with_copy, *refs):
    w_ref = refs[0]
    block_refs = refs[1 : 1 + sources]
    placing_ref, extra_ref = refs[1 + sources : 3 + sources]
    at = 3 + sources + (1 if span else 0)
    out_refs = refs[at : at + blocks]
    held, sem = refs[-2:]
    if with_copy:
        copy = pltpu.make_async_copy(w_ref, refs[at + blocks], sem.at[0])
        copy.start()
    if span:
        start, size = span
        copy = pltpu.make_async_copy(
            refs[at - 1].at[0, :, start : start + size, :], refs[at + blocks], sem.at[0]
        )
        copy.start()
    halves = w_ref.shape[2] // LANES
    count = len(tiles) * VARS
    for r in range(placing_ref.shape[1] // LANES):
        lanes = slice(LANES * r, LANES * (r + 1))
        half = r % halves
        w_lanes = slice(LANES * half, LANES * (half + 1))

        def body(tile, sums):
            start = pl.multiple_of(8 * tile, 8)
            groups = [w_ref[var, pl.ds(start, 8), w_lanes] for var in range(VARS)]
            sums = list(sums)
            for s in range(8):
                rows = [jnp.broadcast_to(group[s : s + 1], (8, LANES)) for group in groups]
                for m, (source, at) in enumerate(tiles):
                    block = block_refs[source][start + s, 8 * at : 8 * at + 8, lanes]
                    for var in range(VARS):
                        q = m * VARS + var
                        sums[q] = sums[q] + block * rows[var]
            return tuple(sums)

        start = tuple(jnp.zeros((8, LANES), jnp.float32) for _ in range(count))
        sums = lax.fori_loop(0, 8, body, start)
        for q in range(count):
            held[8 * q : 8 * q + 8, lanes] = sums[q]

    values = jnp.concatenate([held[...], extra_ref[...]], axis=0)
    total = values.shape[0]
    pieces = jnp.concatenate(split_two(values), axis=0)
    result = lax.dot_general(
        pieces,
        placing_ref[...],
        (((1,), (1,)), ((), ())),
        preferred_element_type=jnp.float32,
    )
    result = result[0:total] + result[total:]
    per = result.shape[1] // blocks
    for g in range(blocks):
        for part in range(per // LANES):
            at = per * g + LANES * part
            out_refs[g][part] = result[:, at : at + LANES]
    if with_copy or span:
        copy.wait()


def project(w, sources, placing, extra, tiles, outputs, load=None, with_copy=False):
    slots = placing.shape[1]
    rows = len(tiles) * VARS * 8
    per = placing.shape[0] // outputs // LANES
    operands = [w, *sources, placing, extra]
    in_specs = [vmem_spec()] * len(operands)
    out_shape = [jax.ShapeDtypeStruct((per, rows + 8, LANES), jnp.float32)] * outputs
    out_specs = [vmem_spec()] * outputs
    span = None
    if load is not None:
        blocks, span = load
        operands.append(in_hbm(blocks))
        in_specs.append(hbm_spec())
        out_shape.append(jax.ShapeDtypeStruct((64, span[1], slots), jnp.float32))
        out_specs.append(vmem_spec())
    if with_copy:
        out_shape.append(jax.ShapeDtypeStruct(w.shape, jnp.float32))
        out_specs.append(pl.BlockSpec(memory_space=pl.ANY))
    results = pl.pallas_call(
        functools.partial(project_kernel, tiles, len(sources), outputs, span, with_copy),
        out_shape=out_shape,
        in_specs=in_specs,
        out_specs=out_specs,
        scratch_shapes=[
            pltpu.VMEM((rows, slots), jnp.float32),
            pltpu.SemaphoreType.DMA((1,)),
        ],
        compiler_params=params(),
        cost_estimate=pl.CostEstimate(
            flops=1000 * 1000 * 1000 * len(tiles),
            bytes_accessed=4 * rows * 64 * slots,
            transcendentals=0,
        ),
        name="project",
    )(*operands)
    return results[:outputs], results[outputs:]


def add_slots(block_refs, firsts, rows, columns):
    result = jnp.zeros((rows, columns), jnp.float32)
    index = lax.broadcasted_iota(jnp.int32, (columns, LANES), 0)
    for number, ref in enumerate(block_refs):
        for g in range(1 if number < firsts else ref.shape[0]):
            local = ref[g, rows : rows + 1, :].astype(jnp.int32)
            spot = (index == local).astype(jnp.float32).astype(jnp.bfloat16)
            for piece in split_two(ref[g, 0:rows, :]):
                result = result + lax.dot_general(
                    piece, spot, (((1,), (1,)), ((), ())), preferred_element_type=jnp.float32
                )
    return result


def receive_x_kernel(count, firsts, *refs):
    out_ref, xa_ref, xb_ref = refs[count:]
    rows, columns = out_ref.shape
    result = add_slots(refs[:count], firsts, rows, columns)
    out_ref[...] = result

    def tile(m, var):
        q = m * VARS + var
        return result[8 * q : 8 * q + 8]

    lower = [jnp.concatenate([tile(0, v), tile(1, v)], axis=0) for v in range(VARS)]
    upper = [jnp.concatenate([tile(2, v), tile(3, v)], axis=0) for v in range(VARS)]
    pack_x(lower, upper, xa_ref, xb_ref)


def receive_rest_kernel(count, firsts, halves, *refs):
    x_ref, out_ref, ya_ref, yb_ref = refs[count:]
    columns = out_ref.shape[2]
    rest = add_slots(refs[:count], firsts, len(REST_TILES) * VARS * 8, columns)
    for var in range(VARS):
        for m, tile in enumerate(X_TILES):
            q = 8 * (m * VARS + var)
            out_ref[var, 8 * tile : 8 * tile + 8, :] = x_ref[q : q + 8, :]
        for m, tile in enumerate(REST_TILES):
            q = 8 * (m * VARS + var)
            out_ref[var, 8 * tile : 8 * tile + 8, :] = rest[q : q + 8]
    pack_y(
        lambda var, a: tile_of(out_ref, var, 2 * a, 0),
        lambda var, a: tile_of(out_ref, var, 2 * a + 1, halves - 1),
        ya_ref,
        yb_ref,
    )


def receive(kernel, operands, shapes, *settings):
    return pl.pallas_call(
        functools.partial(kernel, *settings),
        out_shape=shapes,
        in_specs=[vmem_spec()] * len(operands),
        out_specs=[vmem_spec()] * len(shapes),
        compiler_params=params(),
        cost_estimate=pl.CostEstimate(
            flops=1000 * 1000 * 1000, bytes_accessed=1000 * 1000, transcendentals=0
        ),
        name="receive",
    )(*operands)


def send_chips(values):
    ring = ("gy", "gz")
    count = len(values)
    mine = [values[0]] * count
    for d in range(count - 1, 0, -1):
        pairs = [(s, s ^ (2 * d)) for s in range(2 * count)]
        mine[d] = lax.ppermute(values[d], ring, pairs)
    return mine


def send_cores(mine):
    others = jnp.concatenate([part[1:2] for part in mine], axis=0)
    pairs = [(s, s ^ 1) for s in range(2 * len(mine))]
    return mine + [lax.ppermute(others, ("gy", "gz"), pairs)]


def send_all(values, group, capacity):
    (values,) = values
    blocks, rows, lanes = values.shape
    per = lanes // capacity
    values = values.reshape(blocks, rows, per, capacity).transpose(0, 2, 1, 3)
    values = values.reshape(group, rows, capacity)
    values = lax.all_to_all(values, ("gy", "gz"), split_axis=0, concat_axis=0, tiled=True)
    values = values.reshape(blocks, per, rows, capacity).transpose(0, 2, 1, 3)
    return [values.reshape(blocks, rows, lanes)]


def per_device(
    adj_final, new_states, old_states, owner_device_index, owner_element_index, proj_blocks
):
    columns = adj_final.shape[3]
    slots = proj_blocks.shape[3]
    group = lax.axis_size("gy") * lax.axis_size("gz")
    capacity = max(2, (2 * slots + group - 1) // group)
    begin, states, faces = get_faces(adj_final, new_states)
    received = exchange(faces)
    second, received = section(states, 2, begin, received, 2.0 / 3.0, [], True)

    direct = group in (2, 4, 8) and capacity == LANES
    outputs = group // 2 if direct else 1
    placing, extra = prepare(
        owner_device_index.reshape(1, slots),
        owner_element_index,
        second,
        group,
        capacity,
        direct,
    )
    first, received = section(
        states, 1, second, received, 0.25, [], True, after=[extra]
    )
    result, outer = section(
        states,
        0,
        first,
        received,
        1.0,
        [(begin, 1.0 / 3.0), (second, 0.75)],
        False,
        load=(proj_blocks, ((0, 16), (48, 16))),
    )

    tiles = tuple((0, m) for m in range(4))
    x_out, (inner,) = project(
        result, [outer], placing, extra, tiles, outputs, load=(proj_blocks, (16, 32))
    )
    rest_out, (adj_new,) = project(
        result, [inner], placing, extra, tiles, outputs, with_copy=True
    )
    send = send_chips if direct else lambda out: send_all(out, group, capacity)
    x_in = send(x_out)
    rest_in = send(rest_out)
    firsts = group // 2 if direct else 0
    cross = send_cores if direct else lambda blocks: blocks

    def rows_of(tiles):
        return jax.ShapeDtypeStruct((len(tiles) * VARS * 8, columns), jnp.float32)

    faces = face_shapes(columns)
    x_in = cross(x_in)
    x_part, *x_faces = receive(
        receive_x_kernel, x_in, [rows_of(X_TILES)] + faces[:2], len(x_in), firsts
    )
    xb, xa = exchange_x(x_faces)
    rest_in = cross(rest_in)
    adj_proj, *y_faces = receive(
        receive_rest_kernel,
        rest_in + [x_part],
        [jax.ShapeDtypeStruct((VARS, 64, columns), jnp.float32)] + faces[2:],
        len(rest_in),
        firsts,
        columns // LANES,
    )
    yb, ya = exchange_y(y_faces)
    adj_old = reverse_step(old_states[0], adj_proj, (xa, xb, yb, ya))
    return (adj_new.reshape(adj_final.shape), adj_old.reshape(adj_final.shape))


def solution(mesh):
    in_specs = (
        P("gx", None, None, ("gy", "gz")),
        P("gx", None, None, None, ("gy", "gz")),
        P("gx", None, None, None, ("gy", "gz")),
        P("gx", ("gy", "gz"), None),
        P("gx", ("gy", "gz")),
        P("gx", None, None, ("gy", "gz")),
    )
    out_specs = (P("gx", None, None, ("gy", "gz")), P("gx", None, None, ("gy", "gz")))
    return jax.shard_map(
        per_device, mesh=mesh, in_specs=in_specs, out_specs=out_specs, check_vma=False
    )
```

```python
import functools

import jax
import jax.numpy as jnp
import numpy as np
from jax import lax
from jax.experimental import pallas as pl
from jax.experimental.pallas import tpu as pltpu
from jax.sharding import PartitionSpec as P

ELEMENTS_Z = 64

step_rate = 0.01
lift_scale = 6.0
half_lift = 3.0
vmem_limit = 24 * 1024 * 1024
VARS = 5
LANES = 128


def swapped(value, axis, offset):
    count = lax.axis_size(axis)
    pairs = []
    for source in range(count):
        up = source % 2 == offset
        pairs.append((source, (source + (1 if up else -1)) % count))
    return lax.ppermute(value, axis, pairs)


def even_places():
    along_x = lax.axis_index("gx")
    along_y = lax.axis_index("gy") * lax.axis_size("gz") + lax.axis_index("gz")
    return lax.rem(along_x, 2) == 0, lax.rem(along_y, 2) == 0


def lgl_matrix():
    points = np.array([-1.0, -1.0 / np.sqrt(5.0), 1.0 / np.sqrt(5.0), 1.0])
    factors = np.array(
        [np.prod([points[i] - points[j] for j in range(4) if j != i]) for i in range(4)]
    )
    deriv_table = np.zeros((4, 4))
    for i in range(4):
        for j in range(4):
            if i != j:
                deriv_table[i, j] = factors[i] / (factors[j] * (points[i] - points[j]))
    for i in range(4):
        deriv_table[i, i] = -np.sum(deriv_table[i])
    return deriv_table


face_table = lgl_matrix()
face_table[0, 0] += half_lift
face_table[3, 3] -= half_lift
assert np.max(np.abs(np.diag(face_table))) < 1e-12


def iotas():
    row = lax.broadcasted_iota(jnp.int32, (8, LANES), 0)
    lane = lax.broadcasted_iota(jnp.int32, (8, LANES), 1)
    return row, lane


def by_sublane(row, values):
    out = jnp.full((8, LANES), np.float32(values[7]))
    for s in range(6, -1, -1):
        out = jnp.where(row == s, np.float32(values[s]), out)
    return out


def tile_of(ref, v, i, j):
    lead = v if isinstance(v, tuple) else (v,)
    return ref[lead + (slice(8 * i, 8 * i + 8), slice(LANES * j, LANES * (j + 1)))]


def primitive_state(get):
    inverse = 1.0 / get(0)
    speeds = [get(1 + d) * inverse for d in range(3)]
    kinetic = (
        get(1) * speeds[0] + get(2) * speeds[1] + get(3) * speeds[2]
    )
    energy = get(4)
    pressure = 0.4 * (energy - 0.5 * kinetic)
    return speeds, (energy + pressure) * inverse


def pull_full(speeds, enthalpy, v):
    total = v[0][4] * speeds[0] + v[1][4] * speeds[1] + v[2][4] * speeds[2]
    weight = v[0][1] + v[1][2] + v[2][3] + total
    fifth = 0.2 * weight
    pulled = []
    for d in range(3):
        part = (
            v[d][1] * speeds[0]
            + v[d][2] * speeds[1]
            + v[d][3] * speeds[2]
            + v[d][4] * enthalpy
        )
        pulled.append(part - fifth * speeds[d])
    out = [-(pulled[0] * speeds[0] + pulled[1] * speeds[1] + pulled[2] * speeds[2])]
    for j in range(3):
        moved = (
            v[0][1 + j] * speeds[0] + v[1][1 + j] * speeds[1] + v[2][1 + j] * speeds[2]
        )
        out.append(v[j][0] + moved - fifth * speeds[j] + pulled[j])
    out.append(total + 2.0 * fifth)
    return out


def pull_one(direction, speeds, enthalpy, v):
    own = speeds[direction]
    total = v[4] * own
    fifth = 0.2 * (v[1 + direction] + total)
    pulled = [-fifth * speeds[d] for d in range(3)]
    pulled[direction] = (
        v[1] * speeds[0]
        + v[2] * speeds[1]
        + v[3] * speeds[2]
        + v[4] * enthalpy
        + pulled[direction]
    )
    out = [-(pulled[0] * speeds[0] + pulled[1] * speeds[1] + pulled[2] * speeds[2])]
    for j in range(3):
        moved = v[1 + j] * own - fifth * speeds[j] + pulled[j]
        out.append(v[0] + moved if j == direction else moved)
    out.append(total + 2.0 * fifth)
    return out


def local_kernel(scale, index, extras, halves, spans, *refs):
    state_ref, w_ref = refs[0], refs[1]
    extra_refs = refs[2 : 2 + len(extras)]
    copies = []
    if spans:
        block_ref, out_ref, loaded_ref, sems = refs[2 + len(extras) :]
        at = 0
        for number, (start, size) in enumerate(spans):
            copies.append(
                pltpu.make_async_copy(
                    block_ref.at[0, :, start : start + size, :],
                    loaded_ref.at[:, at : at + size, :],
                    sems.at[number],
                )
            )
            copies[-1].start()
            at += size
    else:
        out_ref = refs[2 + len(extras)]
    row, lane = iotas()
    low_half_rows = row < 4
    low_half_lanes = lane < 64
    z_first = lane % ELEMENTS_Z == 0
    z_last = lane % ELEMENTS_Z == ELEMENTS_Z - 1
    z_shift = {}
    for k in (1, 2, 3, -1, -2, -3):
        column = [
            face_table[s % 4 - k, s % 4] if 0 <= s % 4 - k <= 3 else 0.0 for s in range(8)
        ]
        z_shift[k] = by_sublane(row, column)
    z_low = by_sublane(row, [half_lift if s % 4 == 0 else 0.0 for s in range(8)])
    z_high = by_sublane(row, [-half_lift if s % 4 == 3 else 0.0 for s in range(8)])
    zero = jnp.zeros((8, LANES), jnp.float32)

    for j in range(halves):
        for i in range(8):
            a, t = i // 2, i % 2
            other = 2 * a + 1 - t
            bs = [2 * t + s // 4 for s in range(8)]
            y_same = by_sublane(row, [face_table[2 * (1 - t) + s // 4, bs[s]] for s in range(8)])
            y_swap = by_sublane(row, [face_table[2 * t + 1 - s // 4, bs[s]] for s in range(8)])
            y_both = by_sublane(
                row, [face_table[2 * (1 - t) + 1 - s // 4, bs[s]] for s in range(8)]
            )
            y_face_rows = low_half_rows if t == 0 else jnp.logical_not(low_half_rows)
            y_sign = half_lift if t == 0 else -half_lift
            y_face = jnp.where(y_face_rows, np.float32(y_sign), 0.0)
            count = by_sublane(
                row,
                [
                    lift_scale
                    * ((a in (0, 3)) + (bs[s] in (0, 3)) + (s % 4 in (0, 3)))
                    for s in range(8)
                ],
            )
            v = [[], [], []]
            penalties = []
            for var in range(VARS):
                w = tile_of(w_ref, var, i, j)
                acc = None
                for source in range(4):
                    if source == a:
                        continue
                    term = np.float32(face_table[source, a]) * tile_of(
                        w_ref, var, 2 * source + t, j
                    )
                    acc = term if acc is None else acc + term
                v[0].append(acc)
                pair = tile_of(w_ref, var, other, j)
                pair_swapped = pltpu.roll(pair, 4, 0)
                acc = (
                    y_same * pair
                    + y_swap * pltpu.roll(w, 4, 0)
                    + y_both * pair_swapped
                )
                here = pltpu.roll(pair_swapped, 64, 1)
                if t == 0:
                    before = (
                        pltpu.roll(pltpu.roll(tile_of(w_ref, var, other, j - 1), 4, 0), 64, 1)
                        if j > 0
                        else zero
                    )
                    y_in = jnp.where(low_half_lanes, before, here)
                else:
                    after = (
                        pltpu.roll(pltpu.roll(tile_of(w_ref, var, other, j + 1), 4, 0), 64, 1)
                        if j < halves - 1
                        else zero
                    )
                    y_in = jnp.where(low_half_lanes, here, after)
                y_term = y_face * y_in
                v[1].append(acc + y_term)
                acc = None
                moved = {}
                for k in (1, 2, 3, -1, -2, -3):
                    moved[k] = pltpu.roll(w, k % 8, 0)
                    term = z_shift[k] * moved[k]
                    acc = term if acc is None else acc + term
                below = jnp.where(
                    z_first, pltpu.roll(moved[-3], 65, 1), pltpu.roll(moved[-3], 1, 1)
                )
                above = jnp.where(
                    z_last, pltpu.roll(moved[3], 63, 1), pltpu.roll(moved[3], 127, 1)
                )
                low_term = z_low * below
                high_term = z_high * above
                v[2].append(acc + low_term + high_term)
                y_jump = y_term if t == 0 else -y_term
                penalties.append(
                    count * w - 2.0 * (y_jump + (low_term - high_term))
                )
            speeds, enthalpy = primitive_state(lambda q: tile_of(state_ref, (index, q), i, j))
            pulled = pull_full(speeds, enthalpy, v)
            for var in range(VARS):
                change = (-step_rate * scale) * (pulled[var] + penalties[var])
                base = scale * tile_of(w_ref, var, i, j)
                for ref, factor in zip(extra_refs, extras):
                    base = base + np.float32(factor) * tile_of(ref, var, i, j)
                out_ref[var, 8 * i : 8 * i + 8, LANES * j : LANES * (j + 1)] = base + change
    for copy in copies:
        copy.wait()


def pack_x(lower, upper, xa_ref, xb_ref):
    even_x, _ = even_places()
    for var in range(VARS):
        xa_ref[var] = jnp.where(even_x, upper[var], lower[var])
        xb_ref[var] = jnp.where(even_x, lower[var], upper[var])


def pack_y(low_of, high_of, ya_ref, yb_ref):
    _, even_y = even_places()
    row, lane = iotas()
    low_rows = row < 4
    low_lanes = lane < 64
    for var in range(VARS):
        low = [low_of(var, a) for a in range(4)]
        left = jnp.where(low_rows, low[0], pltpu.roll(low[1], 4, 0))
        right = jnp.where(low_rows, low[2], pltpu.roll(low[3], 4, 0))
        lower = jnp.where(low_lanes, left, pltpu.roll(right, 64, 1))
        high = [high_of(var, a) for a in range(4)]
        left = jnp.where(low_rows, pltpu.roll(high[0], 4, 0), high[1])
        right = jnp.where(low_rows, pltpu.roll(high[2], 4, 0), high[3])
        upper = jnp.where(low_lanes, pltpu.roll(left, 64, 1), right)
        ya_ref[var] = jnp.where(even_y, upper, lower)
        yb_ref[var] = jnp.where(even_y, lower, upper)


def pack_faces(w_ref, halves, xa_ref, xb_ref, ya_ref, yb_ref):
    lower = [w_ref[var, 0:16, :] for var in range(VARS)]
    upper = [w_ref[var, 48:64, :] for var in range(VARS)]
    pack_x(lower, upper, xa_ref, xb_ref)
    pack_y(
        lambda var, a: tile_of(w_ref, var, 2 * a, 0),
        lambda var, a: tile_of(w_ref, var, 2 * a + 1, halves - 1),
        ya_ref,
        yb_ref,
    )


def face_kernel(halves, w_hbm, state_hbm, w_ref, state_ref, *refs):
    sems = refs[-1]
    first = pltpu.make_async_copy(w_hbm.at[0], w_ref, sems.at[0])
    second = pltpu.make_async_copy(state_hbm.at[0], state_ref, sems.at[1])
    first.start()
    second.start()
    first.wait()
    pack_faces(w_ref, halves, *refs[:-1])
    second.wait()


def finish_kernel(
    scale, index, skip, halves, state_ref, base_ref, xa_ref, xb_ref, yb_ref, ya_ref, *outs
):
    outs = outs[skip:]
    out_ref = outs[0]
    even_x, even_y = even_places()
    row, lane = iotas()
    rate = np.float32(-step_rate * scale)
    y_low_mask = jnp.where(jnp.logical_and(row < 4, lane < 64), np.float32(half_lift), 0.0)
    y_high_mask = jnp.where(jnp.logical_and(row >= 4, lane >= 64), np.float32(-half_lift), 0.0)
    for j in range(halves):
        for i in range(8):
            a, t = i // 2, i % 2
            has_x = a in (0, 3)
            has_y = (t == 0 and j == 0) or (t == 1 and j == halves - 1)
            place = (slice(8 * i, 8 * i + 8), slice(LANES * j, LANES * (j + 1)))
            values = [base_ref[(var,) + place] for var in range(VARS)]
            if has_x or has_y:
                speeds, enthalpy = primitive_state(lambda q: tile_of(state_ref, (index, q), i, j))
            if has_x:
                first = jnp.logical_not(even_x) if a == 0 else even_x
                sign = half_lift if a == 0 else -half_lift
                got = [
                    np.float32(sign)
                    * jnp.where(first, tile_of(xa_ref, var, t, j), tile_of(xb_ref, var, t, j))
                    for var in range(VARS)
                ]
                pulled = pull_one(0, speeds, enthalpy, got)
                jump = 2.0 if a == 0 else -2.0
                values = [
                    x + rate * (g - jump * q) for x, g, q in zip(values, pulled, got)
                ]
            if has_y:
                got = []
                for var in range(VARS):
                    first = jnp.logical_not(even_y) if t == 0 else even_y
                    packed = jnp.where(first, ya_ref[var], yb_ref[var])
                    if t == 0:
                        if a >= 2:
                            packed = pltpu.roll(packed, 64, 1)
                        if a % 2 == 1:
                            packed = pltpu.roll(packed, 4, 0)
                        got.append(y_low_mask * packed)
                    else:
                        if a < 2:
                            packed = pltpu.roll(packed, 64, 1)
                        if a % 2 == 0:
                            packed = pltpu.roll(packed, 4, 0)
                        got.append(y_high_mask * packed)
                pulled = pull_one(1, speeds, enthalpy, got)
                jump = 2.0 if t == 0 else -2.0
                values = [
                    x + rate * (g - jump * q) for x, g, q in zip(values, pulled, got)
                ]
            for var in range(VARS):
                out_ref[(var,) + place] = values[var]
    if len(outs) > 1:
        pack_faces(out_ref, halves, *outs[1:])


def vmem_spec():
    return pl.BlockSpec(memory_space=pltpu.VMEM)


def params():
    return pltpu.CompilerParams(vmem_limit_bytes=vmem_limit)


def face_shapes(columns):
    return [
        jax.ShapeDtypeStruct((VARS, 16, columns), jnp.float32),
        jax.ShapeDtypeStruct((VARS, 16, columns), jnp.float32),
        jax.ShapeDtypeStruct((VARS, 8, LANES), jnp.float32),
        jax.ShapeDtypeStruct((VARS, 8, LANES), jnp.float32),
    ]


def in_hbm(x):
    return pltpu.with_memory_space_constraint(x, pltpu.HBM)


def hbm_spec():
    return pl.BlockSpec(memory_space=pltpu.HBM)


def get_faces(w, states):
    columns = w.shape[3]
    shapes = [
        jax.ShapeDtypeStruct(w.shape[1:], jnp.float32),
        jax.ShapeDtypeStruct(states.shape[1:], jnp.float32),
    ] + face_shapes(columns)
    begin, states, *faces = pl.pallas_call(
        functools.partial(face_kernel, columns // LANES),
        out_shape=shapes,
        in_specs=[hbm_spec()] * 2,
        out_specs=[vmem_spec()] * len(shapes),
        scratch_shapes=[pltpu.SemaphoreType.DMA((2,))],
        compiler_params=params(),
        name="faces",
    )(in_hbm(w), in_hbm(states))
    return begin, states, faces


def prepare_kernel(group, direct, owner_ref, local_ref, after_ref, placing_ref, extra_ref):
    del after_ref
    places, slots = placing_ref.shape
    capacity = places // group
    target = owner_ref[...]
    if direct:
        here = lax.axis_index("gy") * lax.axis_size("gz") + lax.axis_index("gz")
        target = jnp.bitwise_xor(target, here)
    owner = lax.broadcasted_iota(jnp.int32, (group, slots), 0)
    named = jnp.where(owner == target, np.float32(1), np.float32(0))
    earlier = jnp.where(
        lax.broadcasted_iota(jnp.int32, (slots, slots), 0)
        < lax.broadcasted_iota(jnp.int32, (slots, slots), 1),
        np.float32(1),
        np.float32(0),
    )
    ranks = jnp.dot(
        named.astype(jnp.bfloat16),
        earlier.astype(jnp.bfloat16),
        preferred_element_type=jnp.float32,
    )
    rank = jnp.sum(named * ranks, axis=0, keepdims=True).astype(jnp.int32)
    place = target * capacity + rank
    index = lax.broadcasted_iota(jnp.int32, (places, slots), 0)
    placing_ref[...] = jnp.where(index == place, np.float32(1), np.float32(0)).astype(
        jnp.bfloat16
    )
    extra_ref[...] = jnp.broadcast_to(local_ref[...].astype(jnp.float32), extra_ref.shape)


def prepare(owners, local, after, group, capacity, direct):
    slots = local.shape[1]
    return pl.pallas_call(
        functools.partial(prepare_kernel, group, direct),
        out_shape=[
            jax.ShapeDtypeStruct((group * capacity, slots), jnp.bfloat16),
            jax.ShapeDtypeStruct((8, slots), jnp.float32),
        ],
        in_specs=[vmem_spec()] * 3,
        out_specs=[vmem_spec()] * 2,
        compiler_params=params(),
        name="prepare",
    )(owners, local, after)


def exchange_x(faces):
    return swapped(faces[1], "gx", 1), swapped(faces[0], "gx", 0)


def exchange_y(faces):
    ring = ("gy", "gz")
    return swapped(faces[1], ring, 1), swapped(faces[0], ring, 0)


def exchange(faces):
    xb, xa = exchange_x(faces[:2])
    yb, ya = exchange_y(faces[2:])
    return xa, xb, yb, ya


def section(states, index, w, received, scale, extras, with_faces, load=None, after=()):
    columns = w.shape[2]
    halves = columns // LANES
    shape = jax.ShapeDtypeStruct(w.shape, jnp.float32)
    factors = tuple(f for _, f in extras)
    operands = [states, w] + [x for x, _ in extras]
    in_specs = [vmem_spec()] * len(operands)
    out_shape = [shape]
    scratch = []
    spans = ()
    if load is not None:
        blocks, spans = load
        operands.append(in_hbm(blocks))
        in_specs.append(hbm_spec())
        nodes = sum(size for _, size in spans)
        out_shape.append(jax.ShapeDtypeStruct((64, nodes, blocks.shape[3]), jnp.float32))
        scratch = [pltpu.SemaphoreType.DMA((len(spans),))]
    base, *loaded = pl.pallas_call(
        functools.partial(local_kernel, scale, index, factors, halves, spans),
        out_shape=out_shape,
        in_specs=in_specs,
        out_specs=[vmem_spec()] * len(out_shape),
        scratch_shapes=scratch,
        compiler_params=params(),
        cost_estimate=pl.CostEstimate(
            flops=400 * 64 * columns, bytes_accessed=12 * VARS * 64 * columns, transcendentals=0
        ),
        name="local_part",
    )(*operands)
    out_shape = [shape] + (face_shapes(columns) if with_faces else [])
    results = pl.pallas_call(
        functools.partial(finish_kernel, scale, index, len(after), halves),
        out_shape=out_shape,
        in_specs=[vmem_spec()] * (6 + len(after)),
        out_specs=[vmem_spec()] * len(out_shape),
        compiler_params=params(),
        name="finish",
    )(states, base, *received, *after)
    if with_faces:
        results = [results[0], exchange(results[1:])]
    return list(results) + loaded


def reverse_step(states, begin, received):
    second, received = section(states, 2, begin, received, 2.0 / 3.0, [], True)
    first, received = section(states, 1, second, received, 0.25, [], True)
    (result,) = section(
        states, 0, first, received, 1.0, [(begin, 1.0 / 3.0), (second, 0.75)], False
    )
    return result


def split_two(x):
    high = x.astype(jnp.bfloat16)
    low = (x - high.astype(jnp.float32)).astype(jnp.bfloat16)
    return high, low


X_TILES = (0, 1, 6, 7)
REST_TILES = (2, 3, 4, 5)


def project_kernel(tiles, sources, blocks, span, with_copy, *refs):
    w_ref = refs[0]
    block_refs = refs[1 : 1 + sources]
    placing_ref, extra_ref = refs[1 + sources : 3 + sources]
    at = 3 + sources + (1 if span else 0)
    out_refs = refs[at : at + blocks]
    held, sem = refs[-2:]
    if with_copy:
        copy = pltpu.make_async_copy(w_ref, refs[at + blocks], sem.at[0])
        copy.start()
    if span:
        start, size = span
        copy = pltpu.make_async_copy(
            refs[at - 1].at[0, :, start : start + size, :], refs[at + blocks], sem.at[0]
        )
        copy.start()
    halves = w_ref.shape[2] // LANES
    count = len(tiles) * VARS
    for r in range(placing_ref.shape[1] // LANES):
        lanes = slice(LANES * r, LANES * (r + 1))
        half = r % halves
        w_lanes = slice(LANES * half, LANES * (half + 1))

        def body(tile, sums):
            start = pl.multiple_of(8 * tile, 8)
            groups = [w_ref[var, pl.ds(start, 8), w_lanes] for var in range(VARS)]
            sums = list(sums)
            for s in range(8):
                rows = [jnp.broadcast_to(group[s : s + 1], (8, LANES)) for group in groups]
                for m, (source, at) in enumerate(tiles):
                    block = block_refs[source][start + s, 8 * at : 8 * at + 8, lanes]
                    for var in range(VARS):
                        q = m * VARS + var
                        sums[q] = sums[q] + block * rows[var]
            return tuple(sums)

        start = tuple(jnp.zeros((8, LANES), jnp.float32) for _ in range(count))
        sums = lax.fori_loop(0, 8, body, start)
        for q in range(count):
            held[8 * q : 8 * q + 8, lanes] = sums[q]

    values = jnp.concatenate([held[...], extra_ref[...]], axis=0)
    total = values.shape[0]
    pieces = jnp.concatenate(split_two(values), axis=0)
    result = lax.dot_general(
        pieces,
        placing_ref[...],
        (((1,), (1,)), ((), ())),
        preferred_element_type=jnp.float32,
    )
    result = result[0:total] + result[total:]
    per = result.shape[1] // blocks
    for g in range(blocks):
        for part in range(per // LANES):
            at = per * g + LANES * part
            out_refs[g][part] = result[:, at : at + LANES]
    if with_copy or span:
        copy.wait()


def project(w, sources, placing, extra, tiles, outputs, load=None, with_copy=False):
    slots = placing.shape[1]
    rows = len(tiles) * VARS * 8
    per = placing.shape[0] // outputs // LANES
    operands = [w, *sources, placing, extra]
    in_specs = [vmem_spec()] * len(operands)
    out_shape = [jax.ShapeDtypeStruct((per, rows + 8, LANES), jnp.float32)] * outputs
    out_specs = [vmem_spec()] * outputs
    span = None
    if load is not None:
        blocks, span = load
        operands.append(in_hbm(blocks))
        in_specs.append(hbm_spec())
        out_shape.append(jax.ShapeDtypeStruct((64, span[1], slots), jnp.float32))
        out_specs.append(vmem_spec())
    if with_copy:
        out_shape.append(jax.ShapeDtypeStruct(w.shape, jnp.float32))
        out_specs.append(pl.BlockSpec(memory_space=pl.ANY))
    results = pl.pallas_call(
        functools.partial(project_kernel, tiles, len(sources), outputs, span, with_copy),
        out_shape=out_shape,
        in_specs=in_specs,
        out_specs=out_specs,
        scratch_shapes=[
            pltpu.VMEM((rows, slots), jnp.float32),
            pltpu.SemaphoreType.DMA((1,)),
        ],
        compiler_params=params(),
        cost_estimate=pl.CostEstimate(
            flops=1000 * 1000 * 1000 * len(tiles),
            bytes_accessed=4 * rows * 64 * slots,
            transcendentals=0,
        ),
        name="project",
    )(*operands)
    return results[:outputs], results[outputs:]


def add_slots(block_refs, firsts, rows, columns):
    result = jnp.zeros((rows, columns), jnp.float32)
    index = lax.broadcasted_iota(jnp.int32, (columns, LANES), 0)
    for number, ref in enumerate(block_refs):
        for g in range(1 if number < firsts else ref.shape[0]):
            local = ref[g, rows : rows + 1, :].astype(jnp.int32)
            spot = (index == local).astype(jnp.float32).astype(jnp.bfloat16)
            for piece in split_two(ref[g, 0:rows, :]):
                result = result + lax.dot_general(
                    piece, spot, (((1,), (1,)), ((), ())), preferred_element_type=jnp.float32
                )
    return result


def receive_x_kernel(count, firsts, *refs):
    out_ref, xa_ref, xb_ref = refs[count:]
    rows, columns = out_ref.shape
    result = add_slots(refs[:count], firsts, rows, columns)
    out_ref[...] = result

    def tile(m, var):
        q = m * VARS + var
        return result[8 * q : 8 * q + 8]

    lower = [jnp.concatenate([tile(0, v), tile(1, v)], axis=0) for v in range(VARS)]
    upper = [jnp.concatenate([tile(2, v), tile(3, v)], axis=0) for v in range(VARS)]
    pack_x(lower, upper, xa_ref, xb_ref)


def receive_rest_kernel(count, firsts, halves, *refs):
    x_ref, out_ref, ya_ref, yb_ref = refs[count:]
    columns = out_ref.shape[2]
    rest = add_slots(refs[:count], firsts, len(REST_TILES) * VARS * 8, columns)
    for var in range(VARS):
        for m, tile in enumerate(X_TILES):
            q = 8 * (m * VARS + var)
            out_ref[var, 8 * tile : 8 * tile + 8, :] = x_ref[q : q + 8, :]
        for m, tile in enumerate(REST_TILES):
            q = 8 * (m * VARS + var)
            out_ref[var, 8 * tile : 8 * tile + 8, :] = rest[q : q + 8]
    pack_y(
        lambda var, a: tile_of(out_ref, var, 2 * a, 0),
        lambda var, a: tile_of(out_ref, var, 2 * a + 1, halves - 1),
        ya_ref,
        yb_ref,
    )


def receive(kernel, operands, shapes, *settings):
    return pl.pallas_call(
        functools.partial(kernel, *settings),
        out_shape=shapes,
        in_specs=[vmem_spec()] * len(operands),
        out_specs=[vmem_spec()] * len(shapes),
        compiler_params=params(),
        cost_estimate=pl.CostEstimate(
            flops=1000 * 1000 * 1000, bytes_accessed=1000 * 1000, transcendentals=0
        ),
        name="receive",
    )(*operands)


def send_chips(values):
    ring = ("gy", "gz")
    count = len(values)
    mine = [values[0]] * count
    for d in range(1, count):
        pairs = [(s, s ^ (2 * d)) for s in range(2 * count)]
        mine[d] = lax.ppermute(values[d], ring, pairs)
    return mine


def send_cores(mine):
    others = jnp.concatenate([part[1:2] for part in mine], axis=0)
    pairs = [(s, s ^ 1) for s in range(2 * len(mine))]
    return mine + [lax.ppermute(others, ("gy", "gz"), pairs)]


def send_all(values, group, capacity):
    (values,) = values
    blocks, rows, lanes = values.shape
    per = lanes // capacity
    values = values.reshape(blocks, rows, per, capacity).transpose(0, 2, 1, 3)
    values = values.reshape(group, rows, capacity)
    values = lax.all_to_all(values, ("gy", "gz"), split_axis=0, concat_axis=0, tiled=True)
    values = values.reshape(blocks, per, rows, capacity).transpose(0, 2, 1, 3)
    return [values.reshape(blocks, rows, lanes)]


def per_device(
    adj_final, new_states, old_states, owner_device_index, owner_element_index, proj_blocks
):
    columns = adj_final.shape[3]
    slots = proj_blocks.shape[3]
    group = lax.axis_size("gy") * lax.axis_size("gz")
    capacity = max(2, (2 * slots + group - 1) // group)
    begin, states, faces = get_faces(adj_final, new_states)
    received = exchange(faces)
    second, received = section(states, 2, begin, received, 2.0 / 3.0, [], True)

    direct = group in (2, 4, 8) and capacity == LANES
    outputs = group // 2 if direct else 1
    placing, extra = prepare(
        owner_device_index.reshape(1, slots),
        owner_element_index,
        second,
        group,
        capacity,
        direct,
    )
    first, received = section(
        states, 1, second, received, 0.25, [], True, after=[extra]
    )
    result, outer = section(
        states,
        0,
        first,
        received,
        1.0,
        [(begin, 1.0 / 3.0), (second, 0.75)],
        False,
        load=(proj_blocks, ((0, 16), (48, 16))),
    )

    tiles = tuple((0, m) for m in range(4))
    x_out, (inner,) = project(
        result, [outer], placing, extra, tiles, outputs, load=(proj_blocks, (16, 32))
    )
    rest_out, (adj_new,) = project(
        result, [inner], placing, extra, tiles, outputs, with_copy=True
    )
    send = send_chips if direct else lambda out: send_all(out, group, capacity)
    x_in = send(x_out)
    rest_in = send(rest_out)
    firsts = group // 2 if direct else 0
    cross = send_cores if direct else lambda blocks: blocks

    def rows_of(tiles):
        return jax.ShapeDtypeStruct((len(tiles) * VARS * 8, columns), jnp.float32)

    faces = face_shapes(columns)
    x_in = cross(x_in)
    x_part, *x_faces = receive(
        receive_x_kernel, x_in, [rows_of(X_TILES)] + faces[:2], len(x_in), firsts
    )
    xb, xa = exchange_x(x_faces)
    rest_in = cross(rest_in)
    adj_proj, *y_faces = receive(
        receive_rest_kernel,
        rest_in + [x_part],
        [jax.ShapeDtypeStruct((VARS, 64, columns), jnp.float32)] + faces[2:],
        len(rest_in),
        firsts,
        columns // LANES,
    )
    yb, ya = exchange_y(y_faces)
    adj_old = reverse_step(old_states[0], adj_proj, (xa, xb, yb, ya))
    return (adj_new.reshape(adj_final.shape), adj_old.reshape(adj_final.shape))


def solution(mesh):
    in_specs = (
        P("gx", None, None, ("gy", "gz")),
        P("gx", None, None, None, ("gy", "gz")),
        P("gx", None, None, None, ("gy", "gz")),
        P("gx", ("gy", "gz"), None),
        P("gx", ("gy", "gz")),
        P("gx", None, None, ("gy", "gz")),
    )
    out_specs = (P("gx", None, None, ("gy", "gz")), P("gx", None, None, ("gy", "gz")))
    return jax.shard_map(
        per_device, mesh=mesh, in_specs=in_specs, out_specs=out_specs, check_vma=False
    )
```
